32 devices in a mesh: grp: 2 (over core), tm: 16 (over z, y, x).
Axes of the slice: x: 2, y: 2, z: 4, core: 2. Of those that a mesh axis runs over, the one named last changes fastest.
Arguments:
- x_start: float32 [512, 128], P(('grp', 'tm')), may hold values from -3 to 3
- y_start: float32 [512, 128], P('tm'), may hold values from 0 to 1
- cost: float32 [512, 128], P(('grp', 'tm')), may hold values from -6 to 6
- rhs: float32 [512, 128], P('tm'), may hold values from -6 to 6
- tiles: float32 [2048, 128, 128], P(('grp', 'tm')), may hold values from -0.375 to 0.375
- tile_rows: int32 [2048], P(('grp', 'tm')), may hold values from 0 to 511, as said below
- tile_cols: int32 [2048], P(('grp', 'tm')), may hold values from 0 to 511, as said below
- tile_count: int32 [32], P(('grp', 'tm')), may hold values from 1 to 64, as said below
- var_class: int32 [512, 128], P(('grp', 'tm')), may hold values from 0 to 7
- lower_table: float32 [8], replicated, may hold values from -1 to -0.2
- upper_table: float32 [8], replicated, may hold values from 0.2 to 1
Outputs:
- primal: float32 [512, 128], P(('grp', 'tm'))
- dual: float32 [512, 128], P('tm')
- primal_mean: float32 [512, 128], P(('grp', 'tm'))
- dual_mean: float32 [512, 128], P('tm')
The draws below stay inside these ranges and needn't reach their ends.
Inputs may be any that keep to these rules, and one draw needn't show every extreme that they name: `tile_cols`: the tile slots of device d (slots d * 64 to (d + 1) * 64 - 1) name only that device's own column blocks d * 16 to (d + 1) * 16 - 1. `tile_rows`: the tile slots of device d = g * 16 + t name only row blocks of time blocks t - 1, t and t + 1 (rows k * 32 to (k + 1) * 32 - 1 belong to time block k). Only the first tile_count[d] slots of device d are live; some device has all 64 slots live.
All inputs are finite; a program needn't handle non-finite values.
Results may differ from the reference program's by a relative error of at most 0.0001.
Values sent between devices are 32-bit elements; how exact they have to be, the bound alone decides.
No kernel may reach another device: no remote copies, remote signals or barrier semaphores. Data moves between devices by JAX's collectives and lax.ppermute only.
A program may use at most 64 MiB of HBM per device.

```python
import jax
import jax.numpy as jnp
from jax import lax

TILE = 128
CB_DEV = 16
RB_DEV = 32
NT_DEV = 64
NCLASS = 8
ITERS = 2
GCB = 256
NCB = 512
NRB = 512
NTILES = 2048
N_GRP = 2


def draw_tile_cols(key, part):
    device_ids = jnp.arange(NTILES, dtype=jnp.int32) // NT_DEV
    offsets = jax.random.randint(key, (NTILES,), 0, CB_DEV, dtype=jnp.int32)
    return device_ids * CB_DEV + offsets


def draw_tile_rows(key, part):
    time_count = GCB // CB_DEV
    own_time = jnp.arange(NTILES, dtype=jnp.int32) // NT_DEV % time_count
    picks = jax.random.randint(key, (NTILES,), 0, 6, dtype=jnp.int32)
    step_by = jnp.where(picks == 0, -1, jnp.where(picks == 1, 1, 0)).astype(jnp.int32)
    block_time = own_time + step_by
    block_time = jnp.where(block_time < 0, 1, block_time)
    block_time = jnp.where(block_time >= time_count, time_count - 2, block_time)
    offsets = jax.random.randint(jax.random.fold_in(key, 3), (NTILES,), 0, RB_DEV, dtype=jnp.int32)
    return block_time * RB_DEV + offsets


def draw_tile_count(key, part):
    device_total = NTILES // NT_DEV
    shifts = jax.random.randint(key, (device_total,), 0, 7, dtype=jnp.int32)
    counts = jnp.maximum(jnp.right_shift(jnp.full((device_total,), NT_DEV, jnp.int32), shifts), 1)
    busiest = jax.random.randint(jax.random.fold_in(key, 7), (), 0, device_total, dtype=jnp.int32)
    return counts.at[busiest].set(NT_DEV)


def with_ends(values, stream_key, least, high):
    longest = values.shape.index(max(values.shape))
    spots = []
    for shift in (0, 1):
        where = [jax.random.randint(jax.random.fold_in(stream_key, axis), (), 0, length) for axis, length in enumerate(values.shape)]
        where[longest] = (where[longest] + shift) % values.shape[longest]
        spots.append(tuple(where))
    return values.at[spots[0]].set(least).at[spots[1]].set(high)


def steps_of(own_key, dims, split, smallest, top_value):
    level = 1.0
    for dim, parts in split:
        steps = jax.random.uniform(jax.random.fold_in(jax.random.fold_in(own_key, 6), dim), (parts,), jnp.float32, smallest / len(split), top_value / len(split))
        level = level * jnp.repeat(jnp.exp(steps), dims[dim] // parts).reshape((-1,) + (1,) * (len(dims) - 1 - dim))
    return level


def centred(own_key, dims, scale, bound, cuts=(), kind=jnp.bfloat16):
    result = jax.random.normal(own_key, dims, jnp.float32) * scale
    if len(cuts) > 0:
        result = steps_of(own_key, dims, cuts, -0.22, 0.18) * result
    return jnp.clip(result, min=-bound, max=bound).astype(kind)


def setup_inputs(seed: int = 0) -> dict:
    seeds = jax.random.split(jax.random.key(seed), 12)
    x_start = centred(seeds[0], (NCB, TILE), 0.5, 3.0, ((0, 32),), jnp.float32)
    y_start = jnp.clip(1.0 * jax.random.uniform(seeds[1], (NRB, TILE), jnp.float32) ** steps_of(seeds[1], (NRB, TILE), ((0, 16),), -0.2, 0.2), 0.0, 1.0)
    cost = centred(seeds[2], (NCB, TILE), 1.0, 6.0, ((0, 32),), jnp.float32)
    rhs = centred(seeds[3], (NRB, TILE), 1.0, 6.0, ((0, 16),), jnp.float32)
    tiles = centred(seeds[4], (NTILES, TILE, TILE), (TILE * NT_DEV * N_GRP // (2 * RB_DEV)) ** -0.5, 0.375, ((0, 32),), jnp.float32)
    tile_rows = draw_tile_rows(jax.random.fold_in(seeds[11], 71), 0)
    tile_cols = draw_tile_cols(jax.random.fold_in(seeds[11], 71), 0)
    tile_count = draw_tile_count(jax.random.fold_in(seeds[11], 71), 0)
    var_class = with_ends(jax.random.randint(seeds[8], (NCB, TILE), 0, NCLASS), jax.random.fold_in(seeds[8], 1), 0, NCLASS - 1).astype(jnp.int32)
    lower_table = jnp.clip(jax.random.uniform(seeds[9], (NCLASS,), jnp.float32, -1.0, -0.2), -1.0, -0.2)
    upper_table = jnp.clip(jax.random.uniform(seeds[10], (NCLASS,), jnp.float32, 0.2, 1.0), 0.2, 1.0)
    return {"x_start": x_start, "y_start": y_start, "cost": cost, "rhs": rhs, "tiles": tiles, "tile_rows": tile_rows, "tile_cols": tile_cols, "tile_count": tile_count, "var_class": var_class, "lower_table": lower_table, "upper_table": upper_table}


primal_step = 0.6
dual_step = 0.6


def reference(x_start, y_start, cost, rhs, tiles, tile_rows, tile_cols, tile_count, var_class, lower_table, upper_table):
    slot_ids = jnp.arange(NT_DEV, dtype=jnp.int32)
    live_mask = (slot_ids[None, :] < tile_count[:, None]).reshape(-1).astype(tiles.dtype)[:, None]
    lower_bound = lower_table[var_class]
    upper_bound = upper_table[var_class]

    def forward(field):
        picked = field[tile_cols]
        product = jnp.einsum("nrc,nc->nr", tiles, picked, precision=lax.Precision.HIGHEST) * live_mask
        return jnp.zeros((NRB, TILE), field.dtype).at[tile_rows].add(product)

    def adjoint(field):
        picked = field[tile_rows]
        product = jnp.einsum("nrc,nr->nc", tiles, picked, precision=lax.Precision.HIGHEST) * live_mask
        return jnp.zeros((NCB, TILE), field.dtype).at[tile_cols].add(product)

    primal = x_start
    dual = y_start
    primal_total = jnp.zeros_like(x_start)
    dual_total = jnp.zeros_like(y_start)
    for iteration in range(ITERS):
        moved = primal - primal_step * (cost - adjoint(dual))
        primal_next = jnp.minimum(jnp.maximum(moved, lower_bound), upper_bound)
        extrapolated = 2.0 * primal_next - primal
        dual_next = jnp.maximum(dual + dual_step * (rhs - forward(extrapolated)), 0.0)
        primal_total = primal_total + primal_next
        dual_total = dual_total + dual_next
        primal = primal_next
        dual = dual_next
    return (primal, dual, primal_total / ITERS, dual_total / ITERS)
```

```python
import functools

import jax
import jax.numpy as jnp
from jax import lax
from jax.experimental import pallas as pl
from jax.experimental.pallas import tpu as pltpu
from jax.sharding import PartitionSpec as P

ITERS = 2
AXES = ("grp", "tm")
primal_step = 0.6
dual_step = 0.6
f32 = jnp.float32
bf16 = jnp.bfloat16


def split(value):
    high = value.astype(bf16)
    return high, (value - high.astype(f32)).astype(bf16)


def prep_kernel(
    chunks,
    tiles,
    rows,
    cols,
    count,
    classes,
    lower_table,
    upper_table,
    packed,
    row_pick,
    row_sum,
    col_pick,
    col_sum,
    lower,
    upper,
    held,
    sems,
):
    total, size = tiles.shape[0], tiles.shape[1]
    step = total // chunks
    copies = []
    for k in range(chunks):
        part = pl.ds(k * step, step)
        copy = pltpu.make_async_copy(tiles.at[part], held.at[part], sems.at[k])
        copy.start()
        copies.append(copy)
    time = lax.axis_index("tm")
    device = lax.axis_index("grp") * lax.axis_size("tm") + time
    slot = lax.broadcasted_iota(jnp.int32, (1, total), 1)
    live = slot < count[0]
    row_total = row_sum.shape[0]
    col_total = col_sum.shape[0]
    local_rows = rows[...] - (time - 1) * (row_total // 3)
    local_cols = cols[...] - device * col_total
    for local, total_out, pick, summed in (
        (local_rows, row_total, row_pick, row_sum),
        (local_cols, col_total, col_pick, col_sum),
    ):
        hit = lax.broadcasted_iota(jnp.int32, (total_out, total), 0) == local
        alive = jnp.where(hit & live, 1.0, 0.0).astype(f32)
        summed[...] = jnp.concatenate([alive, alive], axis=1).astype(bf16)
        pick[...] = jnp.transpose(jnp.where(hit, 1.0, 0.0).astype(f32)).astype(bf16)
    low = jnp.zeros(classes.shape, f32)
    high = jnp.zeros(classes.shape, f32)
    for k in range(lower_table.shape[0]):
        low = jnp.where(classes[...] == k, lower_table[k], low)
        high = jnp.where(classes[...] == k, upper_table[k], high)
    lower[...] = low
    upper[...] = high
    for k in range(chunks):
        copies[k].wait()
        for n in range(k * step, (k + 1) * step):
            tile_high, tile_low = split(held[n])
            lanes = pl.ds(n % 2 * size, size)
            packed[n // 2, pl.ds(0, size), lanes] = tile_high
            packed[n // 2, pl.ds(size, size), lanes] = tile_low


def products(packed, picked_high, picked_low, transposed):
    total, size = picked_high.shape
    row = lax.broadcasted_iota(jnp.int32, (8, size), 0)
    even = row % 2 == 0
    both = jnp.concatenate([even, even], axis=0)
    outs = []
    for q in range(total // 8):
        part = slice(8 * q, 8 * q + 8)
        left = jnp.concatenate([picked_high[part], picked_low[part]], axis=0)
        if transposed:
            zero = jnp.zeros_like(left)
            left = jnp.concatenate(
                [jnp.where(both, left, zero), jnp.where(both, zero, left)], axis=1
            )
        else:
            left = jnp.concatenate([left, left], axis=1)
        left = left.astype(bf16)
        result = jnp.zeros((8, size), f32)
        for j in range(4):
            out = lax.dot_general(
                left,
                packed[4 * q + j],
                (((1,), (1 if transposed else 0,)), ((), ())),
                preferred_element_type=f32,
            )
            out = out[:8] + out[8:]
            if transposed:
                term = out[:, :size] + out[:, size:]
            else:
                term = jnp.where(even, out[:, :size], out[:, size:])
            result = jnp.where(row // 2 == j, term, result)
        outs.append(result)
    return jnp.concatenate(outs, axis=0)


def pick(selector, values):
    size = values.shape[1]
    both = jnp.concatenate(split(values), axis=1)
    out = jnp.dot(selector[...], both, preferred_element_type=f32)
    return out[:, :size], out[:, size:]


def summed(selector, values):
    both = jnp.concatenate(split(values), axis=0)
    return jnp.dot(selector[...], both, preferred_element_type=f32)


def step_kernel(
    packed,
    row_pick,
    row_sum,
    col_pick,
    col_sum,
    lower,
    upper,
    cost,
    primal,
    offset,
    view,
    primal_out,
    window_out,
):
    blocks = offset.shape[0]
    high, low = pick(row_pick, view[...])
    adjoint = summed(col_sum, products(packed, high, low, False))
    moved = primal[...] - primal_step * (cost[...] - adjoint)
    primal_next = jnp.minimum(jnp.maximum(moved, lower[...]), upper[...])
    primal_out[...] = primal_next
    high, low = pick(col_pick, 2.0 * primal_next - primal[...])
    window = summed(row_sum, products(packed, high, low, True)) * (-dual_step)
    window_out[...] = window
    own = pl.ds(blocks, blocks)
    first = (lax.axis_index("grp") == 0).astype(f32)
    window_out[own] = window[blocks : 2 * blocks] + offset[...] * first


def vmem(count):
    return [pl.BlockSpec(memory_space=pltpu.VMEM)] * count


def body(
    groups,
    times,
    x_start,
    y_start,
    cost,
    rhs,
    tiles,
    tile_rows,
    tile_cols,
    tile_count,
    var_class,
    lower_table,
    upper_table,
):
    total, size = tiles.shape[0], tiles.shape[1]
    cols, rows = x_start.shape[0], y_start.shape[0]
    grp, tm = lax.axis_index("grp"), lax.axis_index("tm")
    rising = grp % 2 == 0

    def number(g, t):
        return g * times + t

    def swap(value, bit):
        route = [
            (number(g, t), number(g ^ bit, t)) for g in range(groups) for t in range(times)
        ]
        return lax.ppermute(value, AXES, route)

    def group_sum(value):
        bit = 1
        while bit < groups:
            value = value + swap(value, bit)
            bit *= 2
        return value

    def ring(distance):
        route = []
        for g in range(groups):
            for t in range(times):
                target = t + distance if g % 2 == 0 else t - distance
                if 0 <= target < times:
                    route.append((number(g, t), number(g, target)))
                else:
                    route.append((number(g, t), number(g ^ 1, t)))
        return route

    def back(distance):
        return [(target, source) for source, target in ring(distance)]

    def neighbours(rising_value, falling_value):
        forth = lax.ppermute(rising_value, AXES, ring(1))
        reverse = lax.ppermute(falling_value, AXES, back(1))
        return jnp.where(rising, forth, reverse), jnp.where(rising, reverse, forth)

    chunks = 8
    prepared = pl.pallas_call(
        functools.partial(prep_kernel, chunks),
        out_shape=(
            jax.ShapeDtypeStruct((total // 2, 2 * size, 2 * size), bf16),
            jax.ShapeDtypeStruct((total, 3 * rows), bf16),
            jax.ShapeDtypeStruct((3 * rows, 2 * total), bf16),
            jax.ShapeDtypeStruct((total, cols), bf16),
            jax.ShapeDtypeStruct((cols, 2 * total), bf16),
            jax.ShapeDtypeStruct(x_start.shape, f32),
            jax.ShapeDtypeStruct(x_start.shape, f32),
        ),
        in_specs=[pl.BlockSpec(memory_space=pl.ANY)]
        + vmem(2)
        + [pl.BlockSpec(memory_space=pltpu.SMEM)]
        + vmem(1)
        + [pl.BlockSpec(memory_space=pltpu.SMEM)] * 2,
        out_specs=tuple(vmem(7)),
        scratch_shapes=[
            pltpu.VMEM(tiles.shape, f32),
            pltpu.SemaphoreType.DMA((chunks,)),
        ],
        compiler_params=pltpu.CompilerParams(vmem_limit_bytes=24 << 20),
        cost_estimate=pl.CostEstimate(
            flops=4 * total * size * size,
            bytes_accessed=8 * total * size * size,
            transcendentals=0,
        ),
        name="prep",
    )(
        tiles,
        tile_rows[None, :],
        tile_cols[None, :],
        tile_count,
        var_class,
        lower_table,
        upper_table,
    )

    def step(primal, offset, view):
        return pl.pallas_call(
            step_kernel,
            out_shape=(
                jax.ShapeDtypeStruct(x_start.shape, f32),
                jax.ShapeDtypeStruct((3 * rows, size), f32),
            ),
            in_specs=vmem(11),
            out_specs=tuple(vmem(2)),
            compiler_params=pltpu.CompilerParams(vmem_limit_bytes=24 << 20),
            cost_estimate=pl.CostEstimate(
                flops=8 * total * size * size,
                bytes_accessed=8 * total * size * size,
                transcendentals=0,
            ),
            name="step",
        )(*prepared, cost, primal, offset, view)

    above, below = neighbours(y_start, y_start)
    view = jnp.concatenate([above, y_start, below], axis=0)
    primal = x_start
    dual = y_start
    primal_total = jnp.zeros_like(x_start)
    dual_total = jnp.zeros_like(y_start)
    for iteration in range(ITERS):
        primal, window = step(primal, dual + dual_step * rhs, view)
        window = group_sum(window)
        low, own, high = window[:rows], window[rows : 2 * rows], window[2 * rows :]
        if iteration + 1 < ITERS:
            near = jnp.where(rising, window[rows:], window[: 2 * rows])
            far = jnp.where(rising, high, low)
            near = lax.ppermute(near, AXES, ring(1))
            far = lax.ppermute(far, AXES, ring(2))
            has_near = jnp.where(rising, tm >= 1, tm + 1 < times)
            has_far = jnp.where(rising, tm >= 2, tm + 2 < times)
            part = jnp.where(rising, near[rows:], near[:rows])
            part = jnp.where(has_near, part, 0.0)
            side = jnp.where(rising, near[:rows] + low, near[rows:] + high)
            side = side + jnp.where(has_far, far, 0.0)
            side = jnp.maximum(side, 0.0)
            sent = jnp.concatenate([side, part], axis=0)
            got = swap(sent, 1)
            dual = jnp.maximum(own + (part + got[rows:]), 0.0)
            above = jnp.where(rising, side, got[:rows])
            below = jnp.where(rising, got[:rows], side)
            view = jnp.concatenate([above, dual, below], axis=0)
        else:
            above, below = neighbours(
                jnp.where(rising, high, low), jnp.where(rising, low, high)
            )
            above = jnp.where(tm >= 1, above, 0.0)
            below = jnp.where(tm + 1 < times, below, 0.0)
            dual = jnp.maximum(own + (above + below), 0.0)
        primal_total = primal_total + primal
        dual_total = dual_total + dual
    return (primal, dual, primal_total / ITERS, dual_total / ITERS)


def solution(mesh):
    groups, times = mesh.shape["grp"], mesh.shape["tm"]
    return jax.shard_map(
        functools.partial(body, groups, times),
        mesh=mesh,
        in_specs=(
            P(("grp", "tm"), None),
            P("tm", None),
            P(("grp", "tm"), None),
            P("tm", None),
            P(("grp", "tm"), None, None),
            P(("grp", "tm")),
            P(("grp", "tm")),
            P(("grp", "tm")),
            P(("grp", "tm"), None),
            P(),
            P(),
        ),
        out_specs=(P(("grp", "tm"), None), P("tm", None), P(("grp", "tm"), None), P("tm", None)),
        check_vma=False,
    )
```

```python
import functools

import jax
import jax.numpy as jnp
from jax import lax
from jax.experimental import pallas as pl
from jax.experimental.pallas import tpu as pltpu
from jax.sharding import PartitionSpec as P

ITERS = 2
AXES = ("grp", "tm")
primal_step = 0.6
dual_step = 0.6
f32 = jnp.float32
bf16 = jnp.bfloat16


def split(value):
    high = value.astype(bf16)
    return high, (value - high.astype(f32)).astype(bf16)


def prep_kernel(
    chunks,
    tiles,
    rows,
    cols,
    count,
    classes,
    lower_table,
    upper_table,
    primal,
    cost,
    dual,
    rhs,
    packed,
    row_pick,
    row_sum,
    col_pick,
    col_sum,
    lower,
    upper,
    primal_out,
    cost_out,
    dual_out,
    rhs_out,
    held,
    rows_in,
    cols_in,
    classes_in,
    lower_in,
    upper_in,
    sems,
):
    total, size = tiles.shape[0], tiles.shape[1]
    step = total // chunks
    small = []
    for source, target in (
        (rows, rows_in),
        (cols, cols_in),
        (classes, classes_in),
        (lower_table, lower_in),
        (upper_table, upper_in),
        (primal, primal_out),
        (cost, cost_out),
        (dual, dual_out),
        (rhs, rhs_out),
    ):
        copy = pltpu.make_async_copy(source, target, sems.at[chunks + len(small)])
        copy.start()
        small.append(copy)
    copies = []
    for k in range(chunks):
        part = pl.ds(k * step, step)
        copy = pltpu.make_async_copy(tiles.at[part], held.at[part], sems.at[k])
        copy.start()
        copies.append(copy)
    for copy in small:
        copy.wait()
    time = lax.axis_index("tm")
    device = lax.axis_index("grp") * lax.axis_size("tm") + time
    slot = lax.broadcasted_iota(jnp.int32, (1, total), 1)
    live = slot < count[0]
    row_total = row_sum.shape[0]
    col_total = col_sum.shape[0]
    local_rows = rows_in[...] - (time - 1) * (row_total // 3)
    local_cols = cols_in[...] - device * col_total
    for local, total_out, pick, summed in (
        (local_rows, row_total, row_pick, row_sum),
        (local_cols, col_total, col_pick, col_sum),
    ):
        hit = lax.broadcasted_iota(jnp.int32, (total_out, total), 0) == local
        alive = jnp.where(hit & live, 1.0, 0.0).astype(f32)
        summed[...] = jnp.concatenate([alive, alive], axis=1).astype(bf16)
        pick[...] = jnp.transpose(jnp.where(hit, 1.0, 0.0).astype(f32)).astype(bf16)
    low = jnp.zeros(classes.shape, f32)
    high = jnp.zeros(classes.shape, f32)
    for k in range(lower_table.shape[0]):
        low = jnp.where(classes_in[...] == k, lower_in[k], low)
        high = jnp.where(classes_in[...] == k, upper_in[k], high)
    lower[...] = low
    upper[...] = high
    for k in range(chunks):
        copies[k].wait()
        for n in range(k * step, (k + 1) * step):
            tile_high, tile_low = split(held[n])
            lanes = pl.ds(n % 2 * size, size)
            packed[n // 2, pl.ds(0, size), lanes] = tile_high
            packed[n // 2, pl.ds(size, size), lanes] = tile_low


def products(packed, picked_high, picked_low, transposed):
    total, size = picked_high.shape
    row = lax.broadcasted_iota(jnp.int32, (8, size), 0)
    even = row % 2 == 0
    both = jnp.concatenate([even, even], axis=0)
    outs = []
    for q in range(total // 8):
        part = slice(8 * q, 8 * q + 8)
        left = jnp.concatenate([picked_high[part], picked_low[part]], axis=0)
        if transposed:
            zero = jnp.zeros_like(left)
            left = jnp.concatenate(
                [jnp.where(both, left, zero), jnp.where(both, zero, left)], axis=1
            )
        else:
            left = jnp.concatenate([left, left], axis=1)
        left = left.astype(bf16)
        result = jnp.zeros((8, size), f32)
        for j in range(4):
            out = lax.dot_general(
                left,
                packed[4 * q + j],
                (((1,), (1 if transposed else 0,)), ((), ())),
                preferred_element_type=f32,
            )
            out = out[:8] + out[8:]
            if transposed:
                term = out[:, :size] + out[:, size:]
            else:
                term = jnp.where(even, out[:, :size], out[:, size:])
            result = jnp.where(row // 2 == j, term, result)
        outs.append(result)
    return jnp.concatenate(outs, axis=0)


def pick(selector, values):
    size = values.shape[1]
    both = jnp.concatenate(split(values), axis=1)
    out = jnp.dot(selector[...], both, preferred_element_type=f32)
    return out[:, :size], out[:, size:]


def summed(selector, values):
    both = jnp.concatenate(split(values), axis=0)
    return jnp.dot(selector[...], both, preferred_element_type=f32)


def iterate(state, view, primal, base):
    packed, row_pick, row_sum, col_pick, col_sum, lower, upper, cost = state
    blocks = base.shape[0]
    high, low = pick(row_pick, view)
    adjoint = summed(col_sum, products(packed, high, low, False))
    moved = primal[...] - primal_step * (cost[...] - adjoint)
    primal_next = jnp.minimum(jnp.maximum(moved, lower[...]), upper[...])
    high, low = pick(col_pick, 2.0 * primal_next - primal[...])
    window = summed(row_sum, products(packed, high, low, True)) * (-dual_step)
    first = (lax.axis_index("grp") == 0).astype(f32)
    own = window[blocks : 2 * blocks] + base * first
    window = jnp.concatenate([window[:blocks], own, window[2 * blocks :]], axis=0)
    return primal_next, window


def rises():
    return lax.rem(lax.axis_index("grp"), 2) == 0


def first_kernel(*refs):
    state, (primal, dual, rhs, forth, reverse), (primal_out, window_out) = (
        refs[:8],
        refs[8:13],
        refs[13:],
    )
    rising = rises()
    above = jnp.where(rising, forth[...], reverse[...])
    below = jnp.where(rising, reverse[...], forth[...])
    view = jnp.concatenate([above, dual[...], below], axis=0)
    primal_out[...], window_out[...] = iterate(
        state, view, primal, dual[...] + dual_step * rhs[...]
    )


def fold_kernel(window, other, summed_out, near_out, far_out):
    blocks = far_out.shape[0]
    total = window[...] + other[...]
    summed_out[...] = total
    rising = rises()
    near_out[...] = jnp.where(rising, total[blocks:], total[: 2 * blocks])
    far_out[...] = jnp.where(rising, total[2 * blocks :], total[:blocks])


def side_kernel(window, near, far, sent):
    blocks = far.shape[0]
    rising = rises()
    time, times = lax.axis_index("tm"), lax.axis_size("tm")
    rank = jnp.where(rising, time, times - 1 - time)
    above, own, below = (window[pl.ds(k * blocks, blocks)] for k in range(3))
    first, last = near[pl.ds(0, blocks)], near[pl.ds(blocks, blocks)]
    part = jnp.where(rising, last, first)
    side = jnp.where(rising, first + above, last + below)
    side = side + jnp.where(rank >= 2, far[...], 0.0)
    sent[pl.ds(0, blocks)] = jnp.maximum(side, 0.0)
    sent[pl.ds(blocks, blocks)] = jnp.where(rank >= 1, part, 0.0)


def later_kernel(*refs):
    state, (primal, rhs, total, sent, got), (primal_out, window_out, mean_out, dual_out) = (
        refs[:8],
        refs[8:13],
        refs[13:],
    )
    blocks = rhs.shape[0]
    rising = rises()
    side, part = (sent[pl.ds(k * blocks, blocks)] for k in range(2))
    other, other_part = (got[pl.ds(k * blocks, blocks)] for k in range(2))
    dual = jnp.maximum(total[pl.ds(blocks, blocks)] + (part + other_part), 0.0)
    above = jnp.where(rising, side, other)
    below = jnp.where(rising, other, side)
    view = jnp.concatenate([above, dual, below], axis=0)
    primal_next, window = iterate(state, view, primal, dual + dual_step * rhs[...])
    primal_out[...] = primal_next
    window_out[...] = window
    mean_out[...] = (primal[...] + primal_next) / ITERS
    dual_out[...] = dual


def last_fold_kernel(window, other, own_out, forth_out, reverse_out):
    blocks = own_out.shape[0]
    total = window[...] + other[...]
    own_out[...] = total[blocks : 2 * blocks]
    rising = rises()
    forth_out[...] = jnp.where(rising, total[2 * blocks :], total[:blocks])
    reverse_out[...] = jnp.where(rising, total[:blocks], total[2 * blocks :])


def vmem(count):
    return [pl.BlockSpec(memory_space=pltpu.VMEM)] * count


def body(
    groups,
    times,
    x_start,
    y_start,
    cost,
    rhs,
    tiles,
    tile_rows,
    tile_cols,
    tile_count,
    var_class,
    lower_table,
    upper_table,
):
    total, size = tiles.shape[0], tiles.shape[1]
    cols, rows = x_start.shape[0], y_start.shape[0]
    tm = lax.axis_index("tm")
    rising = lax.rem(lax.axis_index("grp"), 2) == 0

    def number(g, t):
        return g * times + t

    def swap(value, bit):
        route = [
            (number(g, t), number(g ^ bit, t)) for g in range(groups) for t in range(times)
        ]
        return lax.ppermute(value, AXES, route)

    def group_sum(value):
        bit = 1
        while 2 * bit < groups:
            value = value + swap(value, bit)
            bit *= 2
        return value, swap(value, bit)

    def ring(distance):
        route = []
        for g in range(groups):
            for t in range(times):
                target = t + distance if g % 2 == 0 else t - distance
                if 0 <= target < times:
                    route.append((number(g, t), number(g, target)))
                else:
                    route.append((number(g, t), number(g ^ 1, t)))
        return route

    def back(distance):
        return [(target, source) for source, target in ring(distance)]

    def shape(count, kind=f32, width=size):
        return jax.ShapeDtypeStruct((count, width), kind)

    def kernel(code, name, outs, args, limit=1 << 20, passes=0):
        return pl.pallas_call(
            code,
            out_shape=tuple(outs),
            in_specs=vmem(len(args)),
            out_specs=tuple(vmem(len(outs))),
            compiler_params=pltpu.CompilerParams(vmem_limit_bytes=limit),
            cost_estimate=pl.CostEstimate(
                flops=4 * passes * total * size * size,
                bytes_accessed=4 * passes * total * size * size,
                transcendentals=0,
            ),
            name=name,
        )(*args)

    chunks = 8
    inputs = (
        tiles,
        tile_rows[None, :],
        tile_cols[None, :],
        tile_count,
        var_class,
        lower_table,
        upper_table,
        x_start,
        cost,
        y_start,
        rhs,
    )
    forth = lax.ppermute(y_start, AXES, ring(1))
    reverse = lax.ppermute(y_start, AXES, back(1))
    outs = (
        jax.ShapeDtypeStruct((total // 2, 2 * size, 2 * size), bf16),
        shape(total, bf16, 3 * rows),
        shape(3 * rows, bf16, 2 * total),
        shape(total, bf16, cols),
        shape(cols, bf16, 2 * total),
        shape(cols),
        shape(cols),
        shape(cols),
        shape(cols),
        shape(rows),
        shape(rows),
    )
    *selectors, lower, upper, primal, cost, dual, rhs = pl.pallas_call(
        functools.partial(prep_kernel, chunks),
        out_shape=outs,
        in_specs=[
            pl.BlockSpec(memory_space=pltpu.SMEM if value is tile_count else pltpu.HBM)
            for value in inputs
        ],
        out_specs=tuple(vmem(len(outs))),
        scratch_shapes=[
            pltpu.VMEM(tiles.shape, f32),
            pltpu.VMEM((1, total), jnp.int32),
            pltpu.VMEM((1, total), jnp.int32),
            pltpu.VMEM(var_class.shape, jnp.int32),
            pltpu.SMEM(lower_table.shape, f32),
            pltpu.SMEM(upper_table.shape, f32),
            pltpu.SemaphoreType.DMA((chunks + 9,)),
        ],
        compiler_params=pltpu.CompilerParams(vmem_limit_bytes=16 << 20),
        cost_estimate=pl.CostEstimate(
            flops=4 * total * size * size,
            bytes_accessed=8 * total * size * size,
            transcendentals=0,
        ),
        name="prep",
    )(
        *(
            value if value is tile_count else pltpu.with_memory_space_constraint(value, pltpu.HBM)
            for value in inputs
        )
    )
    state = (*selectors, lower, upper, cost)

    primal_1, window = kernel(
        first_kernel,
        "first",
        (shape(cols), shape(3 * rows)),
        (*state, primal, dual, rhs, forth, reverse),
        limit=16 << 20,
        passes=2,
    )
    window, near, far = kernel(
        fold_kernel,
        "fold",
        (shape(3 * rows), shape(2 * rows), shape(rows)),
        group_sum(window),
    )
    near = lax.ppermute(near, AXES, ring(1))
    far = lax.ppermute(far, AXES, ring(2))
    (sent,) = kernel(side_kernel, "side", (shape(2 * rows),), (window, near, far))
    got = swap(sent, 1)
    primal_2, window, primal_mean, dual_1 = kernel(
        later_kernel,
        "later",
        (shape(cols), shape(3 * rows), shape(cols), shape(rows)),
        (*state, primal_1, rhs, window, sent, got),
        limit=16 << 20,
        passes=2,
    )
    own, forth, reverse = kernel(
        last_fold_kernel,
        "last_fold",
        (shape(rows),) * 3,
        group_sum(window),
    )
    forth = lax.ppermute(forth, AXES, ring(1))
    reverse = lax.ppermute(reverse, AXES, back(1))
    above = jnp.where(tm >= 1, jnp.where(rising, forth, reverse), 0.0)
    below = jnp.where(tm + 1 < times, jnp.where(rising, reverse, forth), 0.0)
    dual_2 = jnp.maximum(own + (above + below), 0.0)
    return primal_2, dual_2, primal_mean, (dual_1 + dual_2) / ITERS


def solution(mesh):
    groups, times = mesh.shape["grp"], mesh.shape["tm"]
    return jax.shard_map(
        functools.partial(body, groups, times),
        mesh=mesh,
        in_specs=(
            P(("grp", "tm"), None),
            P("tm", None),
            P(("grp", "tm"), None),
            P("tm", None),
            P(("grp", "tm"), None, None),
            P(("grp", "tm")),
            P(("grp", "tm")),
            P(("grp", "tm")),
            P(("grp", "tm"), None),
            P(),
            P(),
        ),
        out_specs=(P(("grp", "tm"), None), P("tm", None), P(("grp", "tm"), None), P("tm", None)),
        check_vma=False,
    )
```

```python
import functools

import jax
import jax.numpy as jnp
from jax import lax
from jax.experimental import pallas as pl
from jax.experimental.pallas import tpu as pltpu
from jax.sharding import PartitionSpec as P


ITERS = 2
AXES = ("grp", "tm")
primal_step = 0.6
dual_step = 0.6
f32 = jnp.float32
bf16 = jnp.bfloat16


def split(value):
    high = value.astype(bf16)
    return high, (value - high.astype(f32)).astype(bf16)


def prep_kernel(
    chunks,
    tiles,
    rows,
    cols,
    count,
    classes,
    lower_table,
    upper_table,
    primal,
    cost,
    dual,
    rhs,
    packed,
    row_pick,
    row_sum,
    col_pick,
    col_sum,
    lower,
    upper,
    primal_out,
    cost_out,
    dual_out,
    rhs_out,
    held,
    rows_in,
    cols_in,
    classes_in,
    lower_in,
    upper_in,
    sems,
):
    total, size = tiles.shape[0], tiles.shape[1]
    step = total // chunks
    small = []
    for source, target in (
        (rows, rows_in),
        (cols, cols_in),
        (classes, classes_in),
        (lower_table, lower_in),
        (upper_table, upper_in),
        (primal, primal_out),
        (cost, cost_out),
        (dual, dual_out),
        (rhs, rhs_out),
    ):
        copy = pltpu.make_async_copy(source, target, sems.at[chunks + len(small)])
        copy.start()
        small.append(copy)
    copies = []
    for k in range(chunks):
        part = pl.ds(k * step, step)
        copy = pltpu.make_async_copy(tiles.at[part], held.at[part], sems.at[k])
        copy.start()
        copies.append(copy)
    for copy in small:
        copy.wait()
    time = lax.axis_index("tm")
    device = lax.axis_index("grp") * lax.axis_size("tm") + time
    slot = lax.broadcasted_iota(jnp.int32, (1, total), 1)
    live = slot < count[0]
    row_total = row_sum.shape[0]
    col_total = col_sum.shape[0]
    local_rows = rows_in[...] - (time - 1) * (row_total // 3)
    local_cols = cols_in[...] - device * col_total
    for local, total_out, pick, summed in (
        (local_rows, row_total, row_pick, row_sum),
        (local_cols, col_total, col_pick, col_sum),
    ):
        hit = lax.broadcasted_iota(jnp.int32, (total_out, total), 0) == local
        alive = jnp.where(hit & live, 1.0, 0.0).astype(f32)
        summed[...] = jnp.concatenate([alive, alive], axis=1).astype(bf16)
        pick[...] = jnp.transpose(jnp.where(hit, 1.0, 0.0).astype(f32)).astype(bf16)
    low = jnp.zeros(classes.shape, f32)
    high = jnp.zeros(classes.shape, f32)
    for k in range(lower_table.shape[0]):
        low = jnp.where(classes_in[...] == k, lower_in[k], low)
        high = jnp.where(classes_in[...] == k, upper_in[k], high)
    lower[...] = low
    upper[...] = high
    for k in range(chunks):
        copies[k].wait()
        for n in range(k * step, (k + 1) * step):
            tile_high, tile_low = split(held[n])
            lanes = pl.ds(n % 2 * size, size)
            packed[n // 2, pl.ds(0, size), lanes] = tile_high
            packed[n // 2, pl.ds(size, size), lanes] = tile_low


def products(packed, picked_high, picked_low, transposed):
    total, size = picked_high.shape
    row = lax.broadcasted_iota(jnp.int32, (8, size), 0)
    even = row % 2 == 0
    both = jnp.concatenate([even, even], axis=0)
    outs = []
    for q in range(total // 8):
        part = slice(8 * q, 8 * q + 8)
        left = jnp.concatenate([picked_high[part], picked_low[part]], axis=0)
        if transposed:
            zero = jnp.zeros_like(left)
            left = jnp.concatenate(
                [jnp.where(both, left, zero), jnp.where(both, zero, left)], axis=1
            )
        else:
            left = jnp.concatenate([left, left], axis=1)
        left = left.astype(bf16)
        result = jnp.zeros((8, size), f32)
        for j in range(4):
            out = lax.dot_general(
                left,
                packed[4 * q + j],
                (((1,), (1 if transposed else 0,)), ((), ())),
                preferred_element_type=f32,
            )
            out = out[:8] + out[8:]
            if transposed:
                term = out[:, :size] + out[:, size:]
            else:
                term = jnp.where(even, out[:, :size], out[:, size:])
            result = jnp.where(row // 2 == j, term, result)
        outs.append(result)
    return jnp.concatenate(outs, axis=0)


def pick(selector, values):
    size = values.shape[1]
    both = jnp.concatenate(split(values), axis=1)
    out = jnp.dot(selector[...], both, preferred_element_type=f32)
    return out[:, :size], out[:, size:]


def summed(selector, values):
    both = jnp.concatenate(split(values), axis=0)
    return jnp.dot(selector[...], both, preferred_element_type=f32)


def iterate(state, view, primal, base):
    packed, row_pick, row_sum, col_pick, col_sum, lower, upper, cost = state
    blocks = base.shape[0]
    high, low = pick(row_pick, view)
    adjoint = summed(col_sum, products(packed, high, low, False))
    moved = primal[...] - primal_step * (cost[...] - adjoint)
    primal_next = jnp.minimum(jnp.maximum(moved, lower[...]), upper[...])
    high, low = pick(col_pick, 2.0 * primal_next - primal[...])
    window = summed(row_sum, products(packed, high, low, True)) * (-dual_step)
    first = (lax.axis_index("grp") == 0).astype(f32)
    own = window[blocks : 2 * blocks] + base * first
    window = jnp.concatenate([window[:blocks], own, window[2 * blocks :]], axis=0)
    return primal_next, window


def rises():
    return lax.rem(lax.axis_index("grp"), 2) == 0


def first_kernel(*refs):
    state, (primal, dual, rhs, forth, reverse), (primal_out, window_out) = (
        refs[:8],
        refs[8:13],
        refs[13:],
    )
    even = lax.rem(lax.axis_index("tm"), 2) == 0
    above = jnp.where(even, forth[...], reverse[...])
    below = jnp.where(even, reverse[...], forth[...])
    view = jnp.concatenate([above, dual[...], below], axis=0)
    primal_out[...], window_out[...] = iterate(
        state, view, primal, dual[...] + dual_step * rhs[...]
    )


def fold_kernel(window, other, summed_out, near_out, far_out):
    blocks = far_out.shape[0]
    total = window[...] + other[...]
    summed_out[...] = total
    rising = rises()
    near_out[...] = jnp.where(rising, total[blocks:], total[: 2 * blocks])
    far_out[...] = jnp.where(rising, total[2 * blocks :], total[:blocks])


def side_kernel(window, near, far, sent):
    blocks = far.shape[0]
    rising = rises()
    time, times = lax.axis_index("tm"), lax.axis_size("tm")
    rank = jnp.where(rising, time, times - 1 - time)
    above, _, below = (window[pl.ds(k * blocks, blocks)] for k in range(3))
    first, last = near[pl.ds(0, blocks)], near[pl.ds(blocks, blocks)]
    part = jnp.where(rising, last, first)
    side = jnp.where(rising, first + above, last + below)
    side = side + jnp.where(rank >= 2, far[...], 0.0)
    sent[pl.ds(0, blocks)] = jnp.maximum(side, 0.0)
    sent[pl.ds(blocks, blocks)] = jnp.where(rank >= 1, part, 0.0)


def later_kernel(*refs):
    state, (primal, rhs, total, sent, got), (primal_out, window_out, mean_out, dual_out) = (
        refs[:8],
        refs[8:13],
        refs[13:],
    )
    blocks = rhs.shape[0]
    rising = rises()
    side, part = (sent[pl.ds(k * blocks, blocks)] for k in range(2))
    other, other_part = (got[pl.ds(k * blocks, blocks)] for k in range(2))
    dual = jnp.maximum(total[pl.ds(blocks, blocks)] + (part + other_part), 0.0)
    above = jnp.where(rising, side, other)
    below = jnp.where(rising, other, side)
    view = jnp.concatenate([above, dual, below], axis=0)
    primal_next, window = iterate(state, view, primal, dual + dual_step * rhs[...])
    primal_out[...] = primal_next
    window_out[...] = window
    mean_out[...] = (primal[...] + primal_next) / ITERS
    dual_out[...] = dual


def last_fold_kernel(window, other, own_out, forth_out, reverse_out):
    blocks = own_out.shape[0]
    total = window[...] + other[...]
    own_out[...] = total[blocks : 2 * blocks]
    even = lax.rem(lax.axis_index("tm"), 2) == 0
    forth_out[...] = jnp.where(even, total[:blocks], total[2 * blocks :])
    reverse_out[...] = jnp.where(even, total[2 * blocks :], total[:blocks])


def vmem(count):
    return [pl.BlockSpec(memory_space=pltpu.VMEM)] * count


def body(
    groups,
    times,
    x_start,
    y_start,
    cost,
    rhs,
    tiles,
    tile_rows,
    tile_cols,
    tile_count,
    var_class,
    lower_table,
    upper_table,
):
    total, size = tiles.shape[0], tiles.shape[1]
    cols, rows = x_start.shape[0], y_start.shape[0]
    tm = lax.axis_index("tm")

    def number(g, t):
        return g * times + t

    def swap(value, bit):
        route = [
            (number(g, t), number(g ^ bit, t)) for g in range(groups) for t in range(times)
        ]
        return lax.ppermute(value, AXES, route)

    def group_sum(value):
        bit = 1
        while 2 * bit < groups:
            value = value + swap(value, bit)
            bit *= 2
        return value, swap(value, bit)

    def ring(distance):
        route = []
        for g in range(groups):
            for t in range(times):
                target = t + distance if g % 2 == 0 else t - distance
                if 0 <= target < times:
                    route.append((number(g, t), number(g, target)))
                else:
                    route.append((number(g, t), number(g ^ 1, t)))
        return route

    def pairs(odd):
        route = []
        for g in range(groups):
            for t in range(times):
                target = t + 1 if (t + odd) % 2 == 0 else t - 1
                if 0 <= target < times:
                    route.append((number(g, t), number(g, target)))
                else:
                    route.append((number(g, t), number(g ^ 1, t)))
        return route

    def exchange(odd, even):
        odd = lax.ppermute(odd, AXES, pairs(1))
        even = lax.ppermute(even, AXES, pairs(0))
        return odd, even

    def shape(count, kind=f32, width=size):
        return jax.ShapeDtypeStruct((count, width), kind)

    def kernel(code, outs, args, limit=1 << 20, passes=0):
        return pl.pallas_call(
            code,
            out_shape=tuple(outs),
            in_specs=vmem(len(args)),
            out_specs=tuple(vmem(len(outs))),
            compiler_params=pltpu.CompilerParams(vmem_limit_bytes=limit),
            cost_estimate=pl.CostEstimate(
                flops=4 * passes * total * size * size,
                bytes_accessed=4 * passes * total * size * size,
                transcendentals=0,
            ),
        )(*args)

    chunks = 8
    inputs = (
        tiles,
        tile_rows[None, :],
        tile_cols[None, :],
        tile_count,
        var_class,
        lower_table,
        upper_table,
        x_start,
        cost,
        y_start,
        rhs,
    )
    forth, reverse = exchange(y_start, y_start)
    outs = (
        jax.ShapeDtypeStruct((total // 2, 2 * size, 2 * size), bf16),
        shape(total, bf16, 3 * rows),
        shape(3 * rows, bf16, 2 * total),
        shape(total, bf16, cols),
        shape(cols, bf16, 2 * total),
        shape(cols),
        shape(cols),
        shape(cols),
        shape(cols),
        shape(rows),
        shape(rows),
    )
    *selectors, lower, upper, primal, cost, dual, rhs = pl.pallas_call(
        functools.partial(prep_kernel, chunks),
        out_shape=outs,
        in_specs=[
            pl.BlockSpec(memory_space=pltpu.SMEM if value is tile_count else pltpu.HBM)
            for value in inputs
        ],
        out_specs=tuple(vmem(len(outs))),
        scratch_shapes=[
            pltpu.VMEM(tiles.shape, f32),
            pltpu.VMEM((1, total), jnp.int32),
            pltpu.VMEM((1, total), jnp.int32),
            pltpu.VMEM(var_class.shape, jnp.int32),
            pltpu.SMEM(lower_table.shape, f32),
            pltpu.SMEM(upper_table.shape, f32),
            pltpu.SemaphoreType.DMA((chunks + 9,)),
        ],
        compiler_params=pltpu.CompilerParams(vmem_limit_bytes=16 << 20),
        cost_estimate=pl.CostEstimate(
            flops=4 * total * size * size,
            bytes_accessed=8 * total * size * size,
            transcendentals=0,
        ),
        name="prep",
    )(
        *(
            value if value is tile_count else pltpu.with_memory_space_constraint(value, pltpu.HBM)
            for value in inputs
        )
    )
    state = (*selectors, lower, upper, cost)

    primal_1, window = kernel(
        first_kernel,
        (shape(cols), shape(3 * rows)),
        (*state, primal, dual, rhs, forth, reverse),
        limit=16 << 20,
        passes=2,
    )
    window, near, far = kernel(
        fold_kernel, (shape(3 * rows), shape(2 * rows), shape(rows)), group_sum(window)
    )
    near = lax.ppermute(near, AXES, ring(1))
    far = lax.ppermute(far, AXES, ring(2))
    (sent,) = kernel(side_kernel, (shape(2 * rows),), (window, near, far))
    got = swap(sent, 1)
    primal_2, window, primal_mean, dual_1 = kernel(
        later_kernel,
        (shape(cols), shape(3 * rows), shape(cols), shape(rows)),
        (*state, primal_1, rhs, window, sent, got),
        limit=16 << 20,
        passes=2,
    )
    own, forth, reverse = kernel(
        last_fold_kernel, (shape(rows),) * 3, group_sum(window)
    )
    forth, reverse = exchange(forth, reverse)
    even = lax.rem(tm, 2) == 0
    above = jnp.where(tm >= 1, jnp.where(even, forth, reverse), 0.0)
    below = jnp.where(tm + 1 < times, jnp.where(even, reverse, forth), 0.0)
    dual_2 = jnp.maximum(own + (above + below), 0.0)
    return primal_2, dual_2, primal_mean, (dual_1 + dual_2) / ITERS


def solution(mesh):
    groups, times = mesh.shape["grp"], mesh.shape["tm"]
    return jax.shard_map(
        functools.partial(body, groups, times),
        mesh=mesh,
        in_specs=(
            P(("grp", "tm"), None),
            P("tm", None),
            P(("grp", "tm"), None),
            P("tm", None),
            P(("grp", "tm"), None, None),
            P(("grp", "tm")),
            P(("grp", "tm")),
            P(("grp", "tm")),
            P(("grp", "tm"), None),
            P(),
            P(),
        ),
        out_specs=(P(("grp", "tm"), None), P("tm", None), P(("grp", "tm"), None), P("tm", None)),
        check_vma=False,
    )
```

```python
import functools

import jax
import jax.numpy as jnp
from jax import lax
from jax.experimental import pallas as pl
from jax.experimental.pallas import tpu as pltpu
from jax.sharding import PartitionSpec as P


ITERS = 2
AXES = ("grp", "tm")
primal_step = 0.6
dual_step = 0.6
f32 = jnp.float32
bf16 = jnp.bfloat16


def shares(total):
    return total // 32 * 8, total * 3 // 64 * 8


def split(value):
    high = value.astype(bf16)
    return high, (value - high.astype(f32)).astype(bf16)


def prep_kernel(
    chunks,
    tiles,
    rows,
    cols,
    count,
    classes,
    lower_table,
    upper_table,
    primal,
    cost,
    dual,
    rhs,
    packed,
    plain,
    turned,
    row_pick,
    row_sum,
    col_pick,
    col_sum,
    lower,
    upper,
    primal_out,
    cost_out,
    dual_out,
    rhs_out,
    held,
    rows_in,
    cols_in,
    classes_in,
    lower_in,
    upper_in,
    sems,
):
    total, size = tiles.shape[0], tiles.shape[1]
    kept = held.shape[0]
    step = kept // chunks
    small = []
    for source, target in (
        (rows, rows_in),
        (cols, cols_in),
        (classes, classes_in),
        (lower_table, lower_in),
        (upper_table, upper_in),
        (primal, primal_out),
        (cost, cost_out),
        (dual, dual_out),
        (rhs, rhs_out),
    ):
        copy = pltpu.make_async_copy(source, target, sems.at[chunks + len(small)])
        copy.start()
        small.append(copy)
    direct = pltpu.make_async_copy(
        tiles.at[pl.ds(kept, total - kept)], plain, sems.at[chunks + len(small)]
    )
    direct.start()
    copies = []
    for k in range(chunks):
        part = pl.ds(k * step, step)
        copy = pltpu.make_async_copy(tiles.at[part], held.at[part], sems.at[k])
        copy.start()
        copies.append(copy)
    for copy in small:
        copy.wait()
    time = lax.axis_index("tm")
    device = lax.axis_index("grp") * lax.axis_size("tm") + time
    slot = lax.broadcasted_iota(jnp.int32, (1, total), 1)
    live = slot < count[0]
    row_total = row_sum.shape[0]
    col_total = col_sum.shape[0]
    local_rows = rows_in[...] - (time - 1) * (row_total // 3)
    local_cols = cols_in[...] - device * col_total
    for local, total_out, pick, summed in (
        (local_rows, row_total, row_pick, row_sum),
        (local_cols, col_total, col_pick, col_sum),
    ):
        hit = lax.broadcasted_iota(jnp.int32, (total_out, total), 0) == local
        alive = jnp.where(hit & live, 1.0, 0.0).astype(f32)
        summed[...] = jnp.concatenate([alive, alive], axis=1).astype(bf16)
        pick[...] = jnp.transpose(jnp.where(hit, 1.0, 0.0).astype(f32)).astype(bf16)
    low = jnp.zeros(classes.shape, f32)
    high = jnp.zeros(classes.shape, f32)
    for k in range(lower_table.shape[1]):
        low = jnp.where(classes_in[...] == k, jnp.broadcast_to(lower_in[:, k : k + 1], low.shape), low)
        high = jnp.where(classes_in[...] == k, jnp.broadcast_to(upper_in[:, k : k + 1], low.shape), high)
    lower[...] = low
    upper[...] = high
    direct.wait()
    for n in range(kept, total):
        turned[n - kept] = jnp.transpose(plain[n - kept])
        tile_high, tile_low = split(plain[n - kept])
        packed[n, pl.ds(0, size)] = tile_high
        packed[n, pl.ds(size, size)] = tile_low
    for k in range(chunks):
        copies[k].wait()
        for n in range(k * step, (k + 1) * step):
            tile_high, tile_low = split(held[n])
            packed[n, pl.ds(0, size)] = tile_high
            packed[n, pl.ds(size, size)] = tile_low


def packed_group(packed, high, low, q, transposed):
    size = high.shape[1]
    row = lax.broadcasted_iota(jnp.int32, (8, size), 0)
    even = row % 2 == 0
    part = slice(8 * q, 8 * q + 8)
    left = jnp.concatenate([high[part], low[part]], axis=0)
    if transposed:
        both = jnp.concatenate([even, even], axis=0)
        zero = jnp.zeros_like(left)
        left = jnp.concatenate(
            [jnp.where(both, left, zero), jnp.where(both, zero, left)], axis=1
        )
    else:
        left = jnp.concatenate([left, left], axis=1)
    left = left.astype(bf16)
    result = jnp.zeros((8, size), f32)
    for j in range(4):
        out = lax.dot_general(
            left,
            jnp.concatenate([packed[8 * q + 2 * j + k] for k in range(2)], axis=1),
            (((1,), (1 if transposed else 0,)), ((), ())),
            preferred_element_type=f32,
        )
        out = out[:8] + out[8:]
        if transposed:
            term = out[:, :size] + out[:, size:]
        else:
            term = jnp.where(even, out[:, :size], out[:, size:])
        result = jnp.where(row // 2 == j, term, result)
    return result


def pick(selector, values):
    size = values.shape[1]
    both = jnp.concatenate(split(values), axis=1)
    out = jnp.dot(selector[...], both, preferred_element_type=f32)
    return out[:, :size], out[:, size:]


def interleaved(packed, extra, high, low, transposed, one):
    groups = (packed.shape[0] - extra) // 8
    results = []
    done = 0
    for q in range(groups):
        results.append(packed_group(packed, high, low, q, transposed))
        while done * groups < extra * (q + 1):
            one(done)
            done += 1
    return jnp.concatenate(results, axis=0)


def apply(packed, plain, picker, summer, values, rows, transposed, extra):
    size = plain.shape[1]
    skipped = plain.shape[0] - extra
    high, low = pick(picker, values)
    first = high.shape[0] - extra
    lane = lax.broadcasted_iota(jnp.int32, (size, size), 1)
    turned = [jnp.zeros((size, size), f32)]

    def one(n):
        terms = plain[skipped + n] * jnp.broadcast_to(rows[pl.ds(n, 1)], (size, size))
        turned[0] = jnp.where(lane == n, jnp.sum(terms, axis=1, keepdims=True), turned[0])

    if extra:
        rows[pl.ds(0, extra)] = high[first:] + low[first:]
    main = interleaved(packed, extra, high, low, transposed, one)
    if extra:
        main = jnp.concatenate([main, jnp.transpose(turned[0])[:extra]], axis=0)
    both = jnp.concatenate(split(main), axis=0)
    return jnp.dot(summer[...], both, preferred_element_type=f32)


def iterate(state, view, primal, base, scratch):
    packed, plain, turned, row_pick, row_sum, col_pick, col_sum, lower, upper, cost = state
    blocks = base.shape[0]
    extra = shares(row_pick.shape[0])
    adjoint = apply(packed, turned, row_pick, col_sum, view, scratch[0], False, extra[0])
    moved = primal[...] - primal_step * (cost[...] - adjoint)
    primal_next = jnp.minimum(jnp.maximum(moved, lower[...]), upper[...])
    ahead = 2.0 * primal_next - primal[...]
    window = apply(packed, plain, col_pick, row_sum, ahead, scratch[0], True, extra[1])
    window = window * (-dual_step)
    first = (lax.axis_index("grp") == 0).astype(f32)
    own = window[blocks : 2 * blocks] + base * first
    window = jnp.concatenate([window[:blocks], own, window[2 * blocks :]], axis=0)
    return primal_next, window


def rises():
    return lax.rem(lax.axis_index("grp"), 2) == 0


def first_kernel(*refs):
    state, (primal, dual, rhs, forth, reverse), (primal_out, window_out), scratch = (
        refs[:10],
        refs[10:15],
        refs[15:17],
        refs[17:],
    )
    even = lax.rem(lax.axis_index("tm"), 2) == 0
    above = jnp.where(even, forth[...], reverse[...])
    below = jnp.where(even, reverse[...], forth[...])
    view = jnp.concatenate([above, dual[...], below], axis=0)
    primal_out[...], window_out[...] = iterate(
        state, view, primal, dual[...] + dual_step * rhs[...], scratch
    )


def fold_kernel(window, other, summed_out, near_out, far_out):
    blocks = far_out.shape[0]
    total = window[...] + other[...]
    summed_out[...] = total
    rising = rises()
    near_out[...] = jnp.where(rising, total[blocks:], total[: 2 * blocks])
    far_out[...] = jnp.where(rising, total[2 * blocks :], total[:blocks])


def side_kernel(window, near, far, sent):
    blocks = far.shape[0]
    rising = rises()
    time, times = lax.axis_index("tm"), lax.axis_size("tm")
    rank = jnp.where(rising, time, times - 1 - time)
    above, _, below = (window[pl.ds(k * blocks, blocks)] for k in range(3))
    first, last = near[pl.ds(0, blocks)], near[pl.ds(blocks, blocks)]
    part = jnp.where(rising, last, first)
    side = jnp.where(rising, first + above, last + below)
    side = side + jnp.where(rank >= 2, far[...], 0.0)
    sent[pl.ds(0, blocks)] = jnp.maximum(side, 0.0)
    sent[pl.ds(blocks, blocks)] = jnp.where(rank >= 1, part, 0.0)


def later_kernel(*refs):
    state, (primal, rhs, total, sent, got), outs, scratch = (
        refs[:10],
        refs[10:15],
        refs[15:19],
        refs[19:],
    )
    primal_out, window_out, mean_out, dual_out = outs
    blocks = rhs.shape[0]
    rising = rises()
    side, part = (sent[pl.ds(k * blocks, blocks)] for k in range(2))
    other, other_part = (got[pl.ds(k * blocks, blocks)] for k in range(2))
    dual = jnp.maximum(total[pl.ds(blocks, blocks)] + (part + other_part), 0.0)
    above = jnp.where(rising, side, other)
    below = jnp.where(rising, other, side)
    view = jnp.concatenate([above, dual, below], axis=0)
    primal_next, window = iterate(state, view, primal, dual + dual_step * rhs[...], scratch)
    primal_out[...] = primal_next
    window_out[...] = window
    mean_out[...] = (primal[...] + primal_next) / ITERS
    dual_out[...] = dual


def last_fold_kernel(window, other, own_out, forth_out, reverse_out):
    blocks = own_out.shape[0]
    total = window[...] + other[...]
    own_out[...] = total[blocks : 2 * blocks]
    even = lax.rem(lax.axis_index("tm"), 2) == 0
    forth_out[...] = jnp.where(even, total[:blocks], total[2 * blocks :])
    reverse_out[...] = jnp.where(even, total[2 * blocks :], total[:blocks])


def vmem(count):
    return [pl.BlockSpec(memory_space=pltpu.VMEM)] * count


def body(
    groups,
    times,
    x_start,
    y_start,
    cost,
    rhs,
    tiles,
    tile_rows,
    tile_cols,
    tile_count,
    var_class,
    lower_table,
    upper_table,
):
    total, size = tiles.shape[0], tiles.shape[1]
    cols, rows = x_start.shape[0], y_start.shape[0]
    tm = lax.axis_index("tm")

    def number(g, t):
        return g * times + t

    def swap(value, bit):
        route = [
            (number(g, t), number(g ^ bit, t)) for g in range(groups) for t in range(times)
        ]
        return lax.ppermute(value, AXES, route)

    def group_sum(value):
        bit = 1
        while 2 * bit < groups:
            value = value + swap(value, bit)
            bit *= 2
        return value, swap(value, bit)

    def ring(distance):
        route = []
        for g in range(groups):
            for t in range(times):
                target = t + distance if g % 2 == 0 else t - distance
                if 0 <= target < times:
                    route.append((number(g, t), number(g, target)))
                else:
                    route.append((number(g, t), number(g ^ 1, t)))
        return route

    def pairs(odd):
        route = []
        for g in range(groups):
            for t in range(times):
                target = t + 1 if (t + odd) % 2 == 0 else t - 1
                if 0 <= target < times:
                    route.append((number(g, t), number(g, target)))
                else:
                    route.append((number(g, t), number(g ^ 1, t)))
        return route

    def exchange(odd, even):
        odd = lax.ppermute(odd, AXES, pairs(1))
        even = lax.ppermute(even, AXES, pairs(0))
        return odd, even

    def shape(count, kind=f32, width=size):
        return jax.ShapeDtypeStruct((count, width), kind)

    def kernel(code, outs, args, limit=1 << 20, passes=0, scratch=()):
        return pl.pallas_call(
            code,
            out_shape=tuple(outs),
            in_specs=vmem(len(args)),
            out_specs=tuple(vmem(len(outs))),
            scratch_shapes=scratch,
            compiler_params=pltpu.CompilerParams(vmem_limit_bytes=limit),
            cost_estimate=pl.CostEstimate(
                flops=4 * passes * total * size * size,
                bytes_accessed=4 * passes * total * size * size,
                transcendentals=0,
            ),
        )(*args)

    extra = max(shares(total))
    kept = total - extra
    chunks = kept // 8
    inputs = (
        tiles,
        tile_rows[None, :],
        tile_cols[None, :],
        tile_count,
        var_class,
        lower_table[None, :],
        upper_table[None, :],
        x_start,
        cost,
        y_start,
        rhs,
    )
    forth, reverse = exchange(y_start, y_start)
    outs = (
        jax.ShapeDtypeStruct((total, 2 * size, size), bf16),
        jax.ShapeDtypeStruct((extra, size, size), f32),
        jax.ShapeDtypeStruct((extra, size, size), f32),
        shape(total, bf16, 3 * rows),
        shape(3 * rows, bf16, 2 * total),
        shape(total, bf16, cols),
        shape(cols, bf16, 2 * total),
        shape(cols),
        shape(cols),
        shape(cols),
        shape(cols),
        shape(rows),
        shape(rows),
    )
    *selectors, lower, upper, primal, cost, dual, rhs = pl.pallas_call(
        functools.partial(prep_kernel, chunks),
        out_shape=outs,
        in_specs=[
            pl.BlockSpec(memory_space=pltpu.SMEM if value is tile_count else pltpu.HBM)
            for value in inputs
        ],
        out_specs=tuple(vmem(len(outs))),
        scratch_shapes=[
            pltpu.VMEM((kept, size, size), f32),
            pltpu.VMEM((1, total), jnp.int32),
            pltpu.VMEM((1, total), jnp.int32),
            pltpu.VMEM(var_class.shape, jnp.int32),
            pltpu.VMEM((1, lower_table.shape[0]), f32),
            pltpu.VMEM((1, upper_table.shape[0]), f32),
            pltpu.SemaphoreType.DMA((chunks + 10,)),
        ],
        compiler_params=pltpu.CompilerParams(vmem_limit_bytes=16 << 20),
        cost_estimate=pl.CostEstimate(
            flops=4 * total * size * size,
            bytes_accessed=8 * total * size * size,
            transcendentals=0,
        ),
        name="prep",
    )(
        *(
            value if value is tile_count else pltpu.with_memory_space_constraint(value, pltpu.HBM)
            for value in inputs
        )
    )
    state = (*selectors, lower, upper, cost)
    scratch = [pltpu.VMEM((extra, size), f32)]

    primal_1, window = kernel(
        first_kernel,
        (shape(cols), shape(3 * rows)),
        (*state, primal, dual, rhs, forth, reverse),
        limit=16 << 20,
        passes=2,
        scratch=scratch,
    )
    window, near, far = kernel(
        fold_kernel, (shape(3 * rows), shape(2 * rows), shape(rows)), group_sum(window)
    )
    near = lax.ppermute(near, AXES, ring(1))
    far = lax.ppermute(far, AXES, ring(2))
    (sent,) = kernel(side_kernel, (shape(2 * rows),), (window, near, far))
    got = swap(sent, 1)
    primal_2, window, primal_mean, dual_1 = kernel(
        later_kernel,
        (shape(cols), shape(3 * rows), shape(cols), shape(rows)),
        (*state, primal_1, rhs, window, sent, got),
        limit=16 << 20,
        passes=2,
        scratch=scratch,
    )
    own, forth, reverse = kernel(
        last_fold_kernel, (shape(rows),) * 3, group_sum(window)
    )
    forth, reverse = exchange(forth, reverse)
    even = lax.rem(tm, 2) == 0
    above = jnp.where(tm >= 1, jnp.where(even, forth, reverse), 0.0)
    below = jnp.where(tm + 1 < times, jnp.where(even, reverse, forth), 0.0)
    dual_2 = jnp.maximum(own + (above + below), 0.0)
    return primal_2, dual_2, primal_mean, (dual_1 + dual_2) / ITERS


def solution(mesh):
    groups, times = mesh.shape["grp"], mesh.shape["tm"]
    return jax.shard_map(
        functools.partial(body, groups, times),
        mesh=mesh,
        in_specs=(
            P(("grp", "tm"), None),
            P("tm", None),
            P(("grp", "tm"), None),
            P("tm", None),
            P(("grp", "tm"), None, None),
            P(("grp", "tm")),
            P(("grp", "tm")),
            P(("grp", "tm")),
            P(("grp", "tm"), None),
            P(),
            P(),
        ),
        out_specs=(P(("grp", "tm"), None), P("tm", None), P(("grp", "tm"), None), P("tm", None)),
        check_vma=False,
    )
```

```python
import functools

import jax
import jax.numpy as jnp
from jax import lax
from jax.experimental import pallas as pl
from jax.experimental.pallas import tpu as pltpu
from jax.sharding import PartitionSpec as P


ITERS = 2
AXES = ("grp", "tm")
primal_step = 0.6
dual_step = 0.6
f32 = jnp.float32
bf16 = jnp.bfloat16


def shares(total):
    return total // 32 * 8, total * 3 // 64 * 8


def split(value):
    high = value.astype(bf16)
    return high, (value - high.astype(f32)).astype(bf16)


def prep_kernel(
    chunks,
    tiles,
    rows,
    cols,
    count,
    classes,
    lower_table,
    upper_table,
    primal,
    cost,
    dual,
    rhs,
    packed,
    plain,
    turned,
    row_pick,
    row_sum,
    col_pick,
    col_sum,
    lower,
    upper,
    primal_out,
    cost_out,
    dual_out,
    rhs_out,
    held,
    rows_in,
    cols_in,
    classes_in,
    lower_in,
    upper_in,
    sems,
):
    total, size = tiles.shape[0], tiles.shape[1]
    kept = held.shape[0]
    step = kept // chunks
    small = []
    for source, target in (
        (rows, rows_in),
        (cols, cols_in),
        (classes, classes_in),
        (lower_table, lower_in),
        (upper_table, upper_in),
        (primal, primal_out),
        (cost, cost_out),
        (dual, dual_out),
        (rhs, rhs_out),
    ):
        copy = pltpu.make_async_copy(source, target, sems.at[chunks + len(small)])
        copy.start()
        small.append(copy)
    direct = pltpu.make_async_copy(
        tiles.at[pl.ds(kept, total - kept)], plain, sems.at[chunks + len(small)]
    )
    direct.start()
    copies = []
    for k in range(chunks):
        part = pl.ds(k * step, step)
        copy = pltpu.make_async_copy(tiles.at[part], held.at[part], sems.at[k])
        copy.start()
        copies.append(copy)
    for copy in small:
        copy.wait()
    time = lax.axis_index("tm")
    device = lax.axis_index("grp") * lax.axis_size("tm") + time
    slot = lax.broadcasted_iota(jnp.int32, (1, total), 1)
    live = slot < count[0]
    row_total = row_sum.shape[0]
    col_total = col_sum.shape[0]
    local_rows = rows_in[...] - (time - 1) * (row_total // 3)
    local_cols = cols_in[...] - device * col_total
    for local, total_out, pick, summed in (
        (local_rows, row_total, row_pick, row_sum),
        (local_cols, col_total, col_pick, col_sum),
    ):
        hit = lax.broadcasted_iota(jnp.int32, (total_out, total), 0) == local
        alive = jnp.where(hit & live, 1.0, 0.0).astype(f32)
        summed[...] = jnp.concatenate([alive, alive], axis=1).astype(bf16)
        pick[...] = jnp.transpose(jnp.where(hit, 1.0, 0.0).astype(f32)).astype(bf16)
    low = jnp.zeros(classes.shape, f32)
    high = jnp.zeros(classes.shape, f32)
    for k in range(lower_table.shape[1]):
        low = jnp.where(classes_in[...] == k, jnp.broadcast_to(lower_in[:, k : k + 1], low.shape), low)
        high = jnp.where(classes_in[...] == k, jnp.broadcast_to(upper_in[:, k : k + 1], low.shape), high)
    lower[...] = low
    upper[...] = high
    direct.wait()
    for n in range(kept, total):
        turned[n - kept] = jnp.transpose(plain[n - kept])
        tile_high, tile_low = split(plain[n - kept])
        packed[n, pl.ds(0, size)] = tile_high
        packed[n, pl.ds(size, size)] = tile_low
    for k in range(chunks):
        copies[k].wait()
        for n in range(k * step, (k + 1) * step):
            tile_high, tile_low = split(held[n])
            packed[n, pl.ds(0, size)] = tile_high
            packed[n, pl.ds(size, size)] = tile_low


def packed_group(packed, high, low, q, transposed):
    size = high.shape[1]
    row = lax.broadcasted_iota(jnp.int32, (8, size), 0)
    even = row % 2 == 0
    part = slice(8 * q, 8 * q + 8)
    left = jnp.concatenate([high[part], low[part]], axis=0)
    if transposed:
        both = jnp.concatenate([even, even], axis=0)
        zero = jnp.zeros_like(left)
        left = jnp.concatenate(
            [jnp.where(both, left, zero), jnp.where(both, zero, left)], axis=1
        )
    else:
        left = jnp.concatenate([left, left], axis=1)
    left = left.astype(bf16)
    result = jnp.zeros((8, size), f32)
    for j in range(4):
        out = lax.dot_general(
            left,
            jnp.concatenate([packed[8 * q + 2 * j + k] for k in range(2)], axis=1),
            (((1,), (1 if transposed else 0,)), ((), ())),
            preferred_element_type=f32,
        )
        out = out[:8] + out[8:]
        if transposed:
            term = out[:, :size] + out[:, size:]
        else:
            term = jnp.where(even, out[:, :size], out[:, size:])
        result = jnp.where(row // 2 == j, term, result)
    return result


def pick(selector, values):
    size = values.shape[1]
    both = jnp.concatenate(split(values), axis=1)
    out = jnp.dot(selector[...], both, preferred_element_type=f32)
    return out[:, :size], out[:, size:]


def interleaved(packed, extra, high, low, transposed, one):
    groups = (packed.shape[0] - extra) // 8
    results = []
    done = 0
    for q in range(groups):
        results.append(packed_group(packed, high, low, q, transposed))
        while done * groups < extra * (q + 1):
            one(done)
            done += 1
    return jnp.concatenate(results, axis=0)


def apply(packed, plain, picker, summer, values, rows, transposed, extra):
    size = plain.shape[1]
    skipped = plain.shape[0] - extra
    high, low = pick(picker, values)
    first = high.shape[0] - extra
    lane = lax.broadcasted_iota(jnp.int32, (size, size), 1)
    turned = [jnp.zeros((size, size), f32)]

    def one(n):
        terms = plain[skipped + n] * jnp.broadcast_to(rows[pl.ds(n, 1)], (size, size))
        turned[0] = jnp.where(lane == n, jnp.sum(terms, axis=1, keepdims=True), turned[0])

    if extra:
        rows[pl.ds(0, extra)] = high[first:] + low[first:]
    main = interleaved(packed, extra, high, low, transposed, one)
    if extra:
        main = jnp.concatenate([main, jnp.transpose(turned[0])[:extra]], axis=0)
    both = jnp.concatenate(split(main), axis=0)
    return jnp.dot(summer[...], both, preferred_element_type=f32)


def iterate(state, view, primal, base, scratch):
    packed, plain, turned, row_pick, row_sum, col_pick, col_sum, lower, upper, cost = state
    blocks = base.shape[0]
    extra = shares(row_pick.shape[0])
    adjoint = apply(packed, turned, row_pick, col_sum, view, scratch[0], False, extra[0])
    moved = primal[...] - primal_step * (cost[...] - adjoint)
    primal_next = jnp.minimum(jnp.maximum(moved, lower[...]), upper[...])
    ahead = 2.0 * primal_next - primal[...]
    window = apply(packed, plain, col_pick, row_sum, ahead, scratch[0], True, extra[1])
    window = window * (-dual_step)
    first = (lax.axis_index("grp") == 0).astype(f32)
    own = window[blocks : 2 * blocks] + base * first
    window = jnp.concatenate([window[:blocks], own, window[2 * blocks :]], axis=0)
    return primal_next, window


def rises():
    return lax.rem(lax.axis_index("grp"), 2) == 0


def first_kernel(*refs):
    state, (primal, dual, rhs, forth, reverse), (primal_out, window_out), scratch = (
        refs[:10],
        refs[10:15],
        refs[15:17],
        refs[17:],
    )
    even = lax.rem(lax.axis_index("tm"), 2) == 0
    above = jnp.where(even, forth[...], reverse[...])
    below = jnp.where(even, reverse[...], forth[...])
    view = jnp.concatenate([above, dual[...], below], axis=0)
    primal_out[...], window_out[...] = iterate(
        state, view, primal, dual[...] + dual_step * rhs[...], scratch
    )


def fold_kernel(window, other, summed_out, near_out, far_out):
    blocks = far_out.shape[0]
    total = window[...] + other[...]
    summed_out[...] = total
    rising = rises()
    near_out[...] = jnp.where(rising, total[blocks:], total[: 2 * blocks])
    far_out[...] = jnp.where(rising, total[2 * blocks :], total[:blocks])


def side_kernel(window, near, far, sent):
    blocks = far.shape[0]
    rising = rises()
    time, times = lax.axis_index("tm"), lax.axis_size("tm")
    rank = jnp.where(rising, time, times - 1 - time)
    above, _, below = (window[pl.ds(k * blocks, blocks)] for k in range(3))
    first, last = near[pl.ds(0, blocks)], near[pl.ds(blocks, blocks)]
    part = jnp.where(rising, last, first)
    side = jnp.where(rising, first + above, last + below)
    side = side + jnp.where(rank >= 2, far[...], 0.0)
    sent[pl.ds(0, blocks)] = jnp.maximum(side, 0.0)
    sent[pl.ds(blocks, blocks)] = jnp.where(rank >= 1, part, 0.0)


def later_kernel(*refs):
    state, (primal, rhs, total, sent, got), outs, scratch = (
        refs[:10],
        refs[10:15],
        refs[15:18],
        refs[18:],
    )
    primal_out, window_out, dual_out = outs
    blocks = rhs.shape[0]
    rising = rises()
    side, part = (sent[pl.ds(k * blocks, blocks)] for k in range(2))
    other, other_part = (got[pl.ds(k * blocks, blocks)] for k in range(2))
    dual = jnp.maximum(total[pl.ds(blocks, blocks)] + (part + other_part), 0.0)
    above = jnp.where(rising, side, other)
    below = jnp.where(rising, other, side)
    view = jnp.concatenate([above, dual, below], axis=0)
    primal_next, window = iterate(state, view, primal, dual + dual_step * rhs[...], scratch)
    primal_out[...] = primal_next
    window_out[...] = window
    dual_out[...] = dual


def last_fold_kernel(window, other, own_out, forth_out, reverse_out):
    blocks = own_out.shape[0]
    total = window[...] + other[...]
    own_out[...] = total[blocks : 2 * blocks]
    even = lax.rem(lax.axis_index("tm"), 2) == 0
    forth_out[...] = jnp.where(even, total[:blocks], total[2 * blocks :])
    reverse_out[...] = jnp.where(even, total[2 * blocks :], total[:blocks])


def emit_kernel(before, after, primal_out, mean_out):
    primal_out[...] = after[...]
    mean_out[...] = (before[...] + after[...]) / ITERS


def vmem(count):
    return [pl.BlockSpec(memory_space=pltpu.VMEM)] * count


def body(
    groups,
    times,
    x_start,
    y_start,
    cost,
    rhs,
    tiles,
    tile_rows,
    tile_cols,
    tile_count,
    var_class,
    lower_table,
    upper_table,
):
    total, size = tiles.shape[0], tiles.shape[1]
    cols, rows = x_start.shape[0], y_start.shape[0]
    tm = lax.axis_index("tm")

    def number(g, t):
        return g * times + t

    def swap(value, bit):
        route = [
            (number(g, t), number(g ^ bit, t)) for g in range(groups) for t in range(times)
        ]
        return lax.ppermute(value, AXES, route)

    def group_sum(value):
        bit = 1
        while 2 * bit < groups:
            value = value + swap(value, bit)
            bit *= 2
        return value, swap(value, bit)

    def ring(distance):
        route = []
        for g in range(groups):
            for t in range(times):
                target = t + distance if g % 2 == 0 else t - distance
                if 0 <= target < times:
                    route.append((number(g, t), number(g, target)))
                else:
                    route.append((number(g, t), number(g ^ 1, t)))
        return route

    def pairs(odd):
        route = []
        for g in range(groups):
            for t in range(times):
                target = t + 1 if (t + odd) % 2 == 0 else t - 1
                if 0 <= target < times:
                    route.append((number(g, t), number(g, target)))
                else:
                    route.append((number(g, t), number(g ^ 1, t)))
        return route

    def exchange(odd, even):
        odd = lax.ppermute(odd, AXES, pairs(1))
        even = lax.ppermute(even, AXES, pairs(0))
        return odd, even

    def shape(count, kind=f32, width=size):
        return jax.ShapeDtypeStruct((count, width), kind)

    def kernel(code, outs, args, limit=1 << 20, passes=0, scratch=()):
        return pl.pallas_call(
            code,
            out_shape=tuple(outs),
            in_specs=vmem(len(args)),
            out_specs=tuple(vmem(len(outs))),
            scratch_shapes=scratch,
            compiler_params=pltpu.CompilerParams(vmem_limit_bytes=limit),
            cost_estimate=pl.CostEstimate(
                flops=4 * passes * total * size * size,
                bytes_accessed=4 * passes * total * size * size,
                transcendentals=0,
            ),
        )(*args)

    extra = max(shares(total))
    kept = total - extra
    chunks = kept // 8
    inputs = (
        tiles,
        tile_rows[None, :],
        tile_cols[None, :],
        tile_count,
        var_class,
        lower_table[None, :],
        upper_table[None, :],
        x_start,
        cost,
        y_start,
        rhs,
    )
    forth, reverse = exchange(y_start, y_start)
    outs = (
        jax.ShapeDtypeStruct((total, 2 * size, size), bf16),
        jax.ShapeDtypeStruct((extra, size, size), f32),
        jax.ShapeDtypeStruct((extra, size, size), f32),
        shape(total, bf16, 3 * rows),
        shape(3 * rows, bf16, 2 * total),
        shape(total, bf16, cols),
        shape(cols, bf16, 2 * total),
        shape(cols),
        shape(cols),
        shape(cols),
        shape(cols),
        shape(rows),
        shape(rows),
    )
    *selectors, lower, upper, primal, cost, dual, rhs = pl.pallas_call(
        functools.partial(prep_kernel, chunks),
        out_shape=outs,
        in_specs=[
            pl.BlockSpec(memory_space=pltpu.SMEM if value is tile_count else pltpu.HBM)
            for value in inputs
        ],
        out_specs=tuple(vmem(len(outs))),
        scratch_shapes=[
            pltpu.VMEM((kept, size, size), f32),
            pltpu.VMEM((1, total), jnp.int32),
            pltpu.VMEM((1, total), jnp.int32),
            pltpu.VMEM(var_class.shape, jnp.int32),
            pltpu.VMEM((1, lower_table.shape[0]), f32),
            pltpu.VMEM((1, upper_table.shape[0]), f32),
            pltpu.SemaphoreType.DMA((chunks + 10,)),
        ],
        compiler_params=pltpu.CompilerParams(vmem_limit_bytes=16 << 20),
        cost_estimate=pl.CostEstimate(
            flops=4 * total * size * size,
            bytes_accessed=8 * total * size * size,
            transcendentals=0,
        ),
        name="prep",
    )(
        *(
            value if value is tile_count else pltpu.with_memory_space_constraint(value, pltpu.HBM)
            for value in inputs
        )
    )
    state = (*selectors, lower, upper, cost)
    scratch = [pltpu.VMEM((extra, size), f32)]

    primal_1, window = kernel(
        first_kernel,
        (shape(cols), shape(3 * rows)),
        (*state, primal, dual, rhs, forth, reverse),
        limit=16 << 20,
        passes=2,
        scratch=scratch,
    )
    window, near, far = kernel(
        fold_kernel, (shape(3 * rows), shape(2 * rows), shape(rows)), group_sum(window)
    )
    near = lax.ppermute(near, AXES, ring(1))
    far = lax.ppermute(far, AXES, ring(2))
    (sent,) = kernel(side_kernel, (shape(2 * rows),), (window, near, far))
    got = swap(sent, 1)
    primal_2, window, dual_1 = kernel(
        later_kernel,
        (shape(cols), shape(3 * rows), shape(rows)),
        (*state, primal_1, rhs, window, sent, got),
        limit=16 << 20,
        passes=2,
        scratch=scratch,
    )
    own, forth, reverse = kernel(
        last_fold_kernel, (shape(rows),) * 3, group_sum(window)
    )
    forth, reverse = exchange(forth, reverse)
    primal_2, primal_mean = kernel(
        emit_kernel, (shape(cols), shape(cols)), (primal_1, primal_2)
    )
    even = lax.rem(tm, 2) == 0
    above = jnp.where(tm >= 1, jnp.where(even, forth, reverse), 0.0)
    below = jnp.where(tm + 1 < times, jnp.where(even, reverse, forth), 0.0)
    dual_2 = jnp.maximum(own + (above + below), 0.0)
    return primal_2, dual_2, primal_mean, (dual_1 + dual_2) / ITERS


def solution(mesh):
    groups, times = mesh.shape["grp"], mesh.shape["tm"]
    return jax.shard_map(
        functools.partial(body, groups, times),
        mesh=mesh,
        in_specs=(
            P(("grp", "tm"), None),
            P("tm", None),
            P(("grp", "tm"), None),
            P("tm", None),
            P(("grp", "tm"), None, None),
            P(("grp", "tm")),
            P(("grp", "tm")),
            P(("grp", "tm")),
            P(("grp", "tm"), None),
            P(),
            P(),
        ),
        out_specs=(P(("grp", "tm"), None), P("tm", None), P(("grp", "tm"), None), P("tm", None)),
        check_vma=False,
    )
```

```python
import functools

import jax
import jax.numpy as jnp
from jax import lax
from jax.experimental import pallas as pl
from jax.experimental.pallas import tpu as pltpu
from jax.sharding import PartitionSpec as P


ITERS = 2
AXES = ("grp", "tm")
primal_step = 0.6
dual_step = 0.6
f32 = jnp.float32
bf16 = jnp.bfloat16


def shares(total):
    return total // 32 * 8, total * 3 // 64 * 8


def split(value):
    high = value.astype(bf16)
    return high, (value - high.astype(f32)).astype(bf16)


def prep_kernel(
    chunks,
    tiles,
    rows,
    cols,
    count,
    classes,
    lower_table,
    upper_table,
    primal,
    cost,
    dual,
    rhs,
    packed,
    plain,
    turned,
    row_pick,
    row_sum,
    col_pick,
    col_sum,
    lower,
    upper,
    primal_out,
    cost_out,
    dual_out,
    rhs_out,
    held,
    rows_in,
    cols_in,
    classes_in,
    lower_in,
    upper_in,
    sems,
):
    total, size = tiles.shape[0], tiles.shape[1]
    kept = held.shape[0]
    step = kept // chunks
    small = []
    for source, target in (
        (rows, rows_in),
        (cols, cols_in),
        (classes, classes_in),
        (lower_table, lower_in),
        (upper_table, upper_in),
        (primal, primal_out),
        (cost, cost_out),
        (dual, dual_out),
        (rhs, rhs_out),
    ):
        copy = pltpu.make_async_copy(source, target, sems.at[chunks + len(small)])
        copy.start()
        small.append(copy)
    direct = pltpu.make_async_copy(
        tiles.at[pl.ds(kept, total - kept)], plain, sems.at[chunks + len(small)]
    )
    direct.start()
    copies = []
    for k in range(chunks):
        part = pl.ds(k * step, step)
        copy = pltpu.make_async_copy(tiles.at[part], held.at[part], sems.at[k])
        copy.start()
        copies.append(copy)
    for copy in small:
        copy.wait()
    time = lax.axis_index("tm")
    device = lax.axis_index("grp") * lax.axis_size("tm") + time
    slot = lax.broadcasted_iota(jnp.int32, (1, total), 1)
    live = slot < count[0]
    row_total = row_sum.shape[0]
    col_total = col_sum.shape[0]
    local_rows = rows_in[...] - (time - 1) * (row_total // 3)
    local_cols = cols_in[...] - device * col_total
    for local, total_out, pick, summed in (
        (local_rows, row_total, row_pick, row_sum),
        (local_cols, col_total, col_pick, col_sum),
    ):
        hit = lax.broadcasted_iota(jnp.int32, (total_out, total), 0) == local
        alive = jnp.where(hit & live, 1.0, 0.0).astype(f32)
        summed[...] = jnp.concatenate([alive, alive], axis=1).astype(bf16)
        pick[...] = jnp.transpose(jnp.where(hit, 1.0, 0.0).astype(f32)).astype(bf16)
    low = jnp.zeros(classes.shape, f32)
    high = jnp.zeros(classes.shape, f32)
    for k in range(lower_table.shape[1]):
        low = jnp.where(classes_in[...] == k, jnp.broadcast_to(lower_in[:, k : k + 1], low.shape), low)
        high = jnp.where(classes_in[...] == k, jnp.broadcast_to(upper_in[:, k : k + 1], low.shape), high)
    lower[...] = low
    upper[...] = high
    direct.wait()
    for n in range(kept, total):
        turned[n - kept] = jnp.transpose(plain[n - kept])
        tile_high, tile_low = split(plain[n - kept])
        packed[n, pl.ds(0, size)] = tile_high
        packed[n, pl.ds(size, size)] = tile_low
    for k in range(chunks):
        copies[k].wait()
        for n in range(k * step, (k + 1) * step):
            tile_high, tile_low = split(held[n])
            packed[n, pl.ds(0, size)] = tile_high
            packed[n, pl.ds(size, size)] = tile_low


def packed_group(packed, high, low, q, transposed):
    size = high.shape[1]
    row = lax.broadcasted_iota(jnp.int32, (8, size), 0)
    even = row % 2 == 0
    part = slice(8 * q, 8 * q + 8)
    left = jnp.concatenate([high[part], low[part]], axis=0)
    if transposed:
        both = jnp.concatenate([even, even], axis=0)
        zero = jnp.zeros_like(left)
        left = jnp.concatenate(
            [jnp.where(both, left, zero), jnp.where(both, zero, left)], axis=1
        )
    else:
        left = jnp.concatenate([left, left], axis=1)
    left = left.astype(bf16)
    result = jnp.zeros((8, size), f32)
    for j in range(4):
        out = lax.dot_general(
            left,
            jnp.concatenate([packed[8 * q + 2 * j + k] for k in range(2)], axis=1),
            (((1,), (1 if transposed else 0,)), ((), ())),
            preferred_element_type=f32,
        )
        out = out[:8] + out[8:]
        if transposed:
            term = out[:, :size] + out[:, size:]
        else:
            term = jnp.where(even, out[:, :size], out[:, size:])
        result = jnp.where(row // 2 == j, term, result)
    return result


def pick(selector, values):
    size = values.shape[1]
    both = jnp.concatenate(split(values), axis=1)
    out = jnp.dot(selector[...], both, preferred_element_type=f32)
    return out[:, :size], out[:, size:]


def interleaved(packed, used, extra, high, low, transposed, one):
    groups = (used - extra) // 8
    results = []
    done = 0
    for q in range(groups):
        results.append(packed_group(packed, high, low, q, transposed))
        while done * groups < extra * (q + 1):
            one(done)
            done += 1
    return jnp.concatenate(results, axis=0)


def apply(packed, plain, picker, summer, values, rows, transposed, extra, used):
    size = plain.shape[1]
    skipped = plain.shape[0] - extra
    high, low = pick(picker, values)
    first = high.shape[0] - extra
    lane = lax.broadcasted_iota(jnp.int32, (size, size), 1)
    turned = [jnp.zeros((size, size), f32)]

    def one(n):
        terms = plain[skipped + n] * jnp.broadcast_to(rows[pl.ds(n, 1)], (size, size))
        turned[0] = jnp.where(lane == n, jnp.sum(terms, axis=1, keepdims=True), turned[0])

    if extra:
        rows[pl.ds(0, extra)] = high[first:] + low[first:]
    main = interleaved(packed, used, extra, high, low, transposed, one)
    if extra:
        main = jnp.concatenate([main, jnp.transpose(turned[0])[:extra]], axis=0)
    if used < high.shape[0]:
        blank = jnp.zeros((high.shape[0] - used, size), f32)
        main = jnp.concatenate([main, blank], axis=0)
    both = jnp.concatenate(split(main), axis=0)
    return jnp.dot(summer[...], both, preferred_element_type=f32)


def iterate(state, view, primal, base, scratch, emit):
    *state, count = state
    total = state[0].shape[0]

    @pl.when(count[0] * 2 > total)
    def _():
        emit(*advance(state, view, primal, base, scratch, total, shares(total)))

    @pl.when(count[0] * 2 <= total)
    def _():
        emit(*advance(state, view, primal, base, scratch, total // 2, (0, 0)))


def advance(state, view, primal, base, scratch, used, extra):
    packed, plain, turned, row_pick, row_sum, col_pick, col_sum, lower, upper, cost = state
    blocks = base.shape[0]
    adjoint = apply(packed, turned, row_pick, col_sum, view, scratch[0], False, extra[0], used)
    moved = primal[...] - primal_step * (cost[...] - adjoint)
    primal_next = jnp.minimum(jnp.maximum(moved, lower[...]), upper[...])
    ahead = 2.0 * primal_next - primal[...]
    window = apply(packed, plain, col_pick, row_sum, ahead, scratch[0], True, extra[1], used)
    window = window * (-dual_step)
    first = (lax.axis_index("grp") == 0).astype(f32)
    own = window[blocks : 2 * blocks] + base * first
    window = jnp.concatenate([window[:blocks], own, window[2 * blocks :]], axis=0)
    return primal_next, window


def rises():
    return lax.rem(lax.axis_index("grp"), 2) == 0


def first_kernel(*refs):
    state, (primal, dual, rhs, forth, reverse), (primal_out, window_out), scratch = (
        refs[:11],
        refs[11:16],
        refs[16:18],
        refs[18:],
    )
    even = lax.rem(lax.axis_index("tm"), 2) == 0
    above = jnp.where(even, forth[...], reverse[...])
    below = jnp.where(even, reverse[...], forth[...])
    view = jnp.concatenate([above, dual[...], below], axis=0)

    def emit(primal_next, window):
        primal_out[...] = primal_next
        window_out[...] = window

    iterate(state, view, primal, dual[...] + dual_step * rhs[...], scratch, emit)


def fold_kernel(window, other, summed_out, near_out, far_out):
    blocks = far_out.shape[0]
    total = window[...] + other[...]
    summed_out[...] = total
    rising = rises()
    near_out[...] = jnp.where(rising, total[blocks:], total[: 2 * blocks])
    far_out[...] = jnp.where(rising, total[2 * blocks :], total[:blocks])


def side_kernel(window, near, far, sent):
    blocks = far.shape[0]
    rising = rises()
    time, times = lax.axis_index("tm"), lax.axis_size("tm")
    rank = jnp.where(rising, time, times - 1 - time)
    above, _, below = (window[pl.ds(k * blocks, blocks)] for k in range(3))
    first, last = near[pl.ds(0, blocks)], near[pl.ds(blocks, blocks)]
    part = jnp.where(rising, last, first)
    side = jnp.where(rising, first + above, last + below)
    side = side + jnp.where(rank >= 2, far[...], 0.0)
    sent[pl.ds(0, blocks)] = jnp.maximum(side, 0.0)
    sent[pl.ds(blocks, blocks)] = jnp.where(rank >= 1, part, 0.0)


def later_kernel(*refs):
    state, (primal, rhs, total, sent, got), outs, scratch = (
        refs[:11],
        refs[11:16],
        refs[16:19],
        refs[19:],
    )
    primal_out, window_out, dual_out = outs
    blocks = rhs.shape[0]
    rising = rises()
    side, part = (sent[pl.ds(k * blocks, blocks)] for k in range(2))
    other, other_part = (got[pl.ds(k * blocks, blocks)] for k in range(2))
    dual = jnp.maximum(total[pl.ds(blocks, blocks)] + (part + other_part), 0.0)
    above = jnp.where(rising, side, other)
    below = jnp.where(rising, other, side)
    view = jnp.concatenate([above, dual, below], axis=0)
    dual_out[...] = dual

    def emit(primal_next, window):
        primal_out[...] = primal_next
        window_out[...] = window

    iterate(state, view, primal, dual + dual_step * rhs[...], scratch, emit)


def last_fold_kernel(window, other, own_out, forth_out, reverse_out):
    blocks = own_out.shape[0]
    total = window[...] + other[...]
    own_out[...] = total[blocks : 2 * blocks]
    even = lax.rem(lax.axis_index("tm"), 2) == 0
    forth_out[...] = jnp.where(even, total[:blocks], total[2 * blocks :])
    reverse_out[...] = jnp.where(even, total[2 * blocks :], total[:blocks])


def emit_kernel(before, after, primal_out, mean_out):
    primal_out[...] = after[...]
    mean_out[...] = (before[...] + after[...]) / ITERS


def vmem(count):
    return [pl.BlockSpec(memory_space=pltpu.VMEM)] * count


def body(
    groups,
    times,
    x_start,
    y_start,
    cost,
    rhs,
    tiles,
    tile_rows,
    tile_cols,
    tile_count,
    var_class,
    lower_table,
    upper_table,
):
    total, size = tiles.shape[0], tiles.shape[1]
    cols, rows = x_start.shape[0], y_start.shape[0]
    tm = lax.axis_index("tm")

    def number(g, t):
        return g * times + t

    def swap(value, bit):
        route = [
            (number(g, t), number(g ^ bit, t)) for g in range(groups) for t in range(times)
        ]
        return lax.ppermute(value, AXES, route)

    def group_sum(value):
        bit = 1
        while 2 * bit < groups:
            value = value + swap(value, bit)
            bit *= 2
        return value, swap(value, bit)

    def ring(distance):
        route = []
        for g in range(groups):
            for t in range(times):
                target = t + distance if g % 2 == 0 else t - distance
                if 0 <= target < times:
                    route.append((number(g, t), number(g, target)))
                else:
                    route.append((number(g, t), number(g ^ 1, t)))
        return route

    def pairs(odd):
        route = []
        for g in range(groups):
            for t in range(times):
                target = t + 1 if (t + odd) % 2 == 0 else t - 1
                if 0 <= target < times:
                    route.append((number(g, t), number(g, target)))
                else:
                    route.append((number(g, t), number(g ^ 1, t)))
        return route

    def exchange(odd, even):
        odd = lax.ppermute(odd, AXES, pairs(1))
        even = lax.ppermute(even, AXES, pairs(0))
        return odd, even

    def shape(count, kind=f32, width=size):
        return jax.ShapeDtypeStruct((count, width), kind)

    def kernel(code, outs, args, limit=1 << 20, passes=0, scratch=()):
        return pl.pallas_call(
            code,
            out_shape=tuple(outs),
            in_specs=[
                pl.BlockSpec(memory_space=pltpu.SMEM if value is tile_count else pltpu.VMEM)
                for value in args
            ],
            out_specs=tuple(vmem(len(outs))),
            scratch_shapes=scratch,
            compiler_params=pltpu.CompilerParams(vmem_limit_bytes=limit),
            cost_estimate=pl.CostEstimate(
                flops=4 * passes * total * size * size,
                bytes_accessed=4 * passes * total * size * size,
                transcendentals=0,
            ),
        )(*args)

    extra = max(shares(total))
    kept = total - extra
    chunks = kept // 8
    inputs = (
        tiles,
        tile_rows[None, :],
        tile_cols[None, :],
        tile_count,
        var_class,
        lower_table[None, :],
        upper_table[None, :],
        x_start,
        cost,
        y_start,
        rhs,
    )
    forth, reverse = exchange(y_start, y_start)
    outs = (
        jax.ShapeDtypeStruct((total, 2 * size, size), bf16),
        jax.ShapeDtypeStruct((extra, size, size), f32),
        jax.ShapeDtypeStruct((extra, size, size), f32),
        shape(total, bf16, 3 * rows),
        shape(3 * rows, bf16, 2 * total),
        shape(total, bf16, cols),
        shape(cols, bf16, 2 * total),
        shape(cols),
        shape(cols),
        shape(cols),
        shape(cols),
        shape(rows),
        shape(rows),
    )
    *selectors, lower, upper, primal, cost, dual, rhs = pl.pallas_call(
        functools.partial(prep_kernel, chunks),
        out_shape=outs,
        in_specs=[
            pl.BlockSpec(memory_space=pltpu.SMEM if value is tile_count else pltpu.HBM)
            for value in inputs
        ],
        out_specs=tuple(vmem(len(outs))),
        scratch_shapes=[
            pltpu.VMEM((kept, size, size), f32),
            pltpu.VMEM((1, total), jnp.int32),
            pltpu.VMEM((1, total), jnp.int32),
            pltpu.VMEM(var_class.shape, jnp.int32),
            pltpu.VMEM((1, lower_table.shape[0]), f32),
            pltpu.VMEM((1, upper_table.shape[0]), f32),
            pltpu.SemaphoreType.DMA((chunks + 10,)),
        ],
        compiler_params=pltpu.CompilerParams(vmem_limit_bytes=16 << 20),
        cost_estimate=pl.CostEstimate(
            flops=4 * total * size * size,
            bytes_accessed=8 * total * size * size,
            transcendentals=0,
        ),
        name="prep",
    )(
        *(
            value if value is tile_count else pltpu.with_memory_space_constraint(value, pltpu.HBM)
            for value in inputs
        )
    )
    state = (*selectors, lower, upper, cost, tile_count)
    scratch = [pltpu.VMEM((extra, size), f32)]

    primal_1, window = kernel(
        first_kernel,
        (shape(cols), shape(3 * rows)),
        (*state, primal, dual, rhs, forth, reverse),
        limit=16 << 20,
        passes=2,
        scratch=scratch,
    )
    window, near, far = kernel(
        fold_kernel, (shape(3 * rows), shape(2 * rows), shape(rows)), group_sum(window)
    )
    near = lax.ppermute(near, AXES, ring(1))
    far = lax.ppermute(far, AXES, ring(2))
    (sent,) = kernel(side_kernel, (shape(2 * rows),), (window, near, far))
    got = swap(sent, 1)
    primal_2, window, dual_1 = kernel(
        later_kernel,
        (shape(cols), shape(3 * rows), shape(rows)),
        (*state, primal_1, rhs, window, sent, got),
        limit=16 << 20,
        passes=2,
        scratch=scratch,
    )
    own, forth, reverse = kernel(last_fold_kernel, (shape(rows),) * 3, group_sum(window))
    forth, reverse = exchange(forth, reverse)
    primal_2, primal_mean = kernel(emit_kernel, (shape(cols), shape(cols)), (primal_1, primal_2))
    even = lax.rem(tm, 2) == 0
    above = jnp.where(tm >= 1, jnp.where(even, forth, reverse), 0.0)
    below = jnp.where(tm + 1 < times, jnp.where(even, reverse, forth), 0.0)
    dual_2 = jnp.maximum(own + (above + below), 0.0)
    return primal_2, dual_2, primal_mean, (dual_1 + dual_2) / ITERS


def solution(mesh):
    groups, times = mesh.shape["grp"], mesh.shape["tm"]
    return jax.shard_map(
        functools.partial(body, groups, times),
        mesh=mesh,
        in_specs=(
            P(("grp", "tm"), None),
            P("tm", None),
            P(("grp", "tm"), None),
            P("tm", None),
            P(("grp", "tm"), None, None),
            P(("grp", "tm")),
            P(("grp", "tm")),
            P(("grp", "tm")),
            P(("grp", "tm"), None),
            P(),
            P(),
        ),
        out_specs=(P(("grp", "tm"), None), P("tm", None), P(("grp", "tm"), None), P("tm", None)),
        check_vma=False,
    )
```

```python
import functools

import jax
import jax.numpy as jnp
from jax import lax
from jax.experimental import pallas as pl
from jax.experimental.pallas import tpu as pltpu
from jax.sharding import PartitionSpec as P


ITERS = 2
AXES = ("grp", "tm")
primal_step = 0.6
dual_step = 0.6
f32 = jnp.float32
bf16 = jnp.bfloat16


def shares(total):
    return total // 32 * 8, total * 3 // 64 * 8


def split(value):
    high = value.astype(bf16)
    return high, (value - high.astype(f32)).astype(bf16)


def prep_kernel(
    chunks,
    tiles,
    rows,
    cols,
    count,
    classes,
    lower_table,
    upper_table,
    primal,
    cost,
    dual,
    rhs,
    packed,
    plain,
    turned,
    row_pick,
    row_sum,
    col_pick,
    col_sum,
    lower,
    upper,
    primal_out,
    cost_out,
    dual_out,
    rhs_out,
    held,
    rows_in,
    cols_in,
    classes_in,
    lower_in,
    upper_in,
    sems,
):
    total, size = tiles.shape[0], tiles.shape[1]
    kept = held.shape[0]
    step = kept // chunks
    small = []
    for source, target in (
        (rows, rows_in),
        (cols, cols_in),
        (classes, classes_in),
        (lower_table, lower_in),
        (upper_table, upper_in),
        (primal, primal_out),
        (cost, cost_out),
        (dual, dual_out),
        (rhs, rhs_out),
    ):
        copy = pltpu.make_async_copy(source, target, sems.at[chunks + len(small)])
        copy.start()
        small.append(copy)
    direct = pltpu.make_async_copy(
        tiles.at[pl.ds(kept, total - kept)], plain, sems.at[chunks + len(small)]
    )
    more = count[0] * 2 > total
    pl.when(more)(direct.start)
    copies = []
    for k in range(chunks):
        part = pl.ds(k * step, step)
        copy = pltpu.make_async_copy(tiles.at[part], held.at[part], sems.at[k])
        if 2 * k * step < total:
            copy.start()
        else:
            pl.when(more)(copy.start)
        copies.append(copy)
    for copy in small:
        copy.wait()
    time = lax.axis_index("tm")
    device = lax.axis_index("grp") * lax.axis_size("tm") + time
    slot = lax.broadcasted_iota(jnp.int32, (1, total), 1)
    live = slot < count[0]
    row_total = row_sum.shape[0]
    col_total = col_sum.shape[0]
    local_rows = rows_in[...] - (time - 1) * (row_total // 3)
    local_cols = cols_in[...] - device * col_total
    for local, total_out, pick, summed in (
        (local_rows, row_total, row_pick, row_sum),
        (local_cols, col_total, col_pick, col_sum),
    ):
        hit = lax.broadcasted_iota(jnp.int32, (total_out, total), 0) == local
        alive = jnp.where(hit & live, 1.0, 0.0).astype(f32)
        summed[...] = jnp.concatenate([alive, alive], axis=1).astype(bf16)
        pick[...] = jnp.transpose(jnp.where(hit, 1.0, 0.0).astype(f32)).astype(bf16)
    low = jnp.zeros(classes.shape, f32)
    high = jnp.zeros(classes.shape, f32)
    for k in range(lower_table.shape[1]):
        low = jnp.where(classes_in[...] == k, jnp.broadcast_to(lower_in[:, k : k + 1], low.shape), low)
        high = jnp.where(classes_in[...] == k, jnp.broadcast_to(upper_in[:, k : k + 1], low.shape), high)
    lower[...] = low
    upper[...] = high

    def store(n, tile):
        tile_high, tile_low = split(tile)
        packed[n, pl.ds(0, size)] = tile_high
        packed[n, pl.ds(size, size)] = tile_low

    def finish(k):
        copies[k].wait()
        for n in range(k * step, (k + 1) * step):
            store(n, held[n])

    for k in range(chunks):
        if 2 * k * step < total:
            finish(k)

    @pl.when(more)
    def _():
        direct.wait()
        for n in range(kept, total):
            turned[n - kept] = jnp.transpose(plain[n - kept])
            store(n, plain[n - kept])
        for k in range(chunks):
            if 2 * k * step >= total:
                finish(k)


def packed_group(packed, high, low, q, transposed):
    size = high.shape[1]
    row = lax.broadcasted_iota(jnp.int32, (8, size), 0)
    even = row % 2 == 0
    part = slice(8 * q, 8 * q + 8)
    left = jnp.concatenate([high[part], low[part]], axis=0)
    if transposed:
        both = jnp.concatenate([even, even], axis=0)
        zero = jnp.zeros_like(left)
        left = jnp.concatenate(
            [jnp.where(both, left, zero), jnp.where(both, zero, left)], axis=1
        )
    else:
        left = jnp.concatenate([left, left], axis=1)
    left = left.astype(bf16)
    result = jnp.zeros((8, size), f32)
    for j in range(4):
        out = lax.dot_general(
            left,
            jnp.concatenate([packed[8 * q + 2 * j + k] for k in range(2)], axis=1),
            (((1,), (1 if transposed else 0,)), ((), ())),
            preferred_element_type=f32,
        )
        out = out[:8] + out[8:]
        if transposed:
            term = out[:, :size] + out[:, size:]
        else:
            term = jnp.where(even, out[:, :size], out[:, size:])
        result = jnp.where(row // 2 == j, term, result)
    return result


def pick(selector, values):
    size = values.shape[1]
    both = jnp.concatenate(split(values), axis=1)
    out = jnp.dot(selector[...], both, preferred_element_type=f32)
    return out[:, :size], out[:, size:]


def interleaved(packed, used, extra, high, low, transposed, one):
    groups = (used - extra) // 8
    results = []
    done = 0
    for q in range(groups):
        results.append(packed_group(packed, high, low, q, transposed))
        while done * groups < extra * (q + 1):
            one(done)
            done += 1
    return jnp.concatenate(results, axis=0)


def apply(packed, plain, picker, summer, values, rows, transposed, extra, used):
    size = plain.shape[1]
    skipped = plain.shape[0] - extra
    high, low = pick(picker, values)
    first = high.shape[0] - extra
    lane = lax.broadcasted_iota(jnp.int32, (size, size), 1)
    turned = [jnp.zeros((size, size), f32)]

    def one(n):
        terms = plain[skipped + n] * jnp.broadcast_to(rows[pl.ds(n, 1)], (size, size))
        turned[0] = jnp.where(lane == n, jnp.sum(terms, axis=1, keepdims=True), turned[0])

    if extra:
        rows[pl.ds(0, extra)] = high[first:] + low[first:]
    main = interleaved(packed, used, extra, high, low, transposed, one)
    if extra:
        main = jnp.concatenate([main, jnp.transpose(turned[0])[:extra]], axis=0)
    if used < high.shape[0]:
        blank = jnp.zeros((high.shape[0] - used, size), f32)
        main = jnp.concatenate([main, blank], axis=0)
    both = jnp.concatenate(split(main), axis=0)
    return jnp.dot(summer[...], both, preferred_element_type=f32)


def iterate(state, view, primal, base, scratch, emit):
    *state, count = state
    total = state[0].shape[0]

    @pl.when(count[0] * 2 > total)
    def _():
        emit(*advance(state, view, primal, base, scratch, total, shares(total)))

    @pl.when(count[0] * 2 <= total)
    def _():
        emit(*advance(state, view, primal, base, scratch, total // 2, (0, 0)))


def advance(state, view, primal, base, scratch, used, extra):
    packed, plain, turned, row_pick, row_sum, col_pick, col_sum, lower, upper, cost = state
    blocks = base.shape[0]
    adjoint = apply(packed, turned, row_pick, col_sum, view, scratch[0], False, extra[0], used)
    moved = primal[...] - primal_step * (cost[...] - adjoint)
    primal_next = jnp.minimum(jnp.maximum(moved, lower[...]), upper[...])
    ahead = 2.0 * primal_next - primal[...]
    window = apply(packed, plain, col_pick, row_sum, ahead, scratch[0], True, extra[1], used)
    window = window * (-dual_step)
    first = (lax.axis_index("grp") == 0).astype(f32)
    own = window[blocks : 2 * blocks] + base * first
    window = jnp.concatenate([window[:blocks], own, window[2 * blocks :]], axis=0)
    return primal_next, window


def rises():
    return lax.rem(lax.axis_index("grp"), 2) == 0


def first_kernel(*refs):
    state, (primal, dual, rhs, forth, reverse), (primal_out, window_out), scratch = (
        refs[:11],
        refs[11:16],
        refs[16:18],
        refs[18:],
    )
    even = lax.rem(lax.axis_index("tm"), 2) == 0
    above = jnp.where(even, forth[...], reverse[...])
    below = jnp.where(even, reverse[...], forth[...])
    view = jnp.concatenate([above, dual[...], below], axis=0)

    def emit(primal_next, window):
        primal_out[...] = primal_next
        window_out[...] = window

    iterate(state, view, primal, dual[...] + dual_step * rhs[...], scratch, emit)


def fold_kernel(window, other, summed_out, near_out, far_out):
    blocks = far_out.shape[0]
    total = window[...] + other[...]
    summed_out[...] = total
    rising = rises()
    near_out[...] = jnp.where(rising, total[blocks:], total[: 2 * blocks])
    far_out[...] = jnp.where(rising, total[2 * blocks :], total[:blocks])


def side_kernel(window, near, far, sent):
    blocks = far.shape[0]
    rising = rises()
    time, times = lax.axis_index("tm"), lax.axis_size("tm")
    rank = jnp.where(rising, time, times - 1 - time)
    above, _, below = (window[pl.ds(k * blocks, blocks)] for k in range(3))
    first, last = near[pl.ds(0, blocks)], near[pl.ds(blocks, blocks)]
    part = jnp.where(rising, last, first)
    side = jnp.where(rising, first + above, last + below)
    side = side + jnp.where(rank >= 2, far[...], 0.0)
    sent[pl.ds(0, blocks)] = jnp.maximum(side, 0.0)
    sent[pl.ds(blocks, blocks)] = jnp.where(rank >= 1, part, 0.0)


def later_kernel(*refs):
    state, (primal, rhs, total, sent, got), outs, scratch = (
        refs[:11],
        refs[11:16],
        refs[16:19],
        refs[19:],
    )
    primal_out, window_out, dual_out = outs
    blocks = rhs.shape[0]
    rising = rises()
    side, part = (sent[pl.ds(k * blocks, blocks)] for k in range(2))
    other, other_part = (got[pl.ds(k * blocks, blocks)] for k in range(2))
    dual = jnp.maximum(total[pl.ds(blocks, blocks)] + (part + other_part), 0.0)
    above = jnp.where(rising, side, other)
    below = jnp.where(rising, other, side)
    view = jnp.concatenate([above, dual, below], axis=0)
    dual_out[...] = dual

    def emit(primal_next, window):
        primal_out[...] = primal_next
        window_out[...] = window

    iterate(state, view, primal, dual + dual_step * rhs[...], scratch, emit)


def last_fold_kernel(window, other, own_out, forth_out, reverse_out):
    blocks = own_out.shape[0]
    total = window[...] + other[...]
    own_out[...] = total[blocks : 2 * blocks]
    even = lax.rem(lax.axis_index("tm"), 2) == 0
    forth_out[...] = jnp.where(even, total[:blocks], total[2 * blocks :])
    reverse_out[...] = jnp.where(even, total[2 * blocks :], total[:blocks])


def emit_kernel(before, after, primal_out, mean_out):
    primal_out[...] = after[...]
    mean_out[...] = (before[...] + after[...]) / ITERS


def vmem(count):
    return [pl.BlockSpec(memory_space=pltpu.VMEM)] * count


def body(
    groups,
    times,
    x_start,
    y_start,
    cost,
    rhs,
    tiles,
    tile_rows,
    tile_cols,
    tile_count,
    var_class,
    lower_table,
    upper_table,
):
    total, size = tiles.shape[0], tiles.shape[1]
    cols, rows = x_start.shape[0], y_start.shape[0]
    tm = lax.axis_index("tm")

    def number(g, t):
        return g * times + t

    def swap(value, bit):
        route = [
            (number(g, t), number(g ^ bit, t)) for g in range(groups) for t in range(times)
        ]
        return lax.ppermute(value, AXES, route)

    def group_sum(value):
        bit = 1
        while 2 * bit < groups:
            value = value + swap(value, bit)
            bit *= 2
        return value, swap(value, bit)

    def ring(distance):
        route = []
        for g in range(groups):
            for t in range(times):
                target = t + distance if g % 2 == 0 else t - distance
                if 0 <= target < times:
                    route.append((number(g, t), number(g, target)))
                else:
                    route.append((number(g, t), number(g ^ 1, t)))
        return route

    def pairs(odd):
        route = []
        for g in range(groups):
            for t in range(times):
                target = t + 1 if (t + odd) % 2 == 0 else t - 1
                if 0 <= target < times:
                    route.append((number(g, t), number(g, target)))
                else:
                    route.append((number(g, t), number(g ^ 1, t)))
        return route

    def exchange(odd, even):
        odd = lax.ppermute(odd, AXES, pairs(1))
        even = lax.ppermute(even, AXES, pairs(0))
        return odd, even

    def shape(count, kind=f32, width=size):
        return jax.ShapeDtypeStruct((count, width), kind)

    def kernel(code, outs, args, limit=1 << 20, passes=0, scratch=()):
        return pl.pallas_call(
            code,
            out_shape=tuple(outs),
            in_specs=[
                pl.BlockSpec(memory_space=pltpu.SMEM if value is tile_count else pltpu.VMEM)
                for value in args
            ],
            out_specs=tuple(vmem(len(outs))),
            scratch_shapes=scratch,
            compiler_params=pltpu.CompilerParams(vmem_limit_bytes=limit),
            cost_estimate=pl.CostEstimate(
                flops=4 * passes * total * size * size,
                bytes_accessed=4 * passes * total * size * size,
                transcendentals=0,
            ),
        )(*args)

    extra = max(shares(total))
    kept = total - extra
    chunks = kept // 8
    inputs = (
        tiles,
        tile_rows[None, :],
        tile_cols[None, :],
        tile_count,
        var_class,
        lower_table[None, :],
        upper_table[None, :],
        x_start,
        cost,
        y_start,
        rhs,
    )
    forth, reverse = exchange(y_start, y_start)
    outs = (
        jax.ShapeDtypeStruct((total, 2 * size, size), bf16),
        jax.ShapeDtypeStruct((extra, size, size), f32),
        jax.ShapeDtypeStruct((extra, size, size), f32),
        shape(total, bf16, 3 * rows),
        shape(3 * rows, bf16, 2 * total),
        shape(total, bf16, cols),
        shape(cols, bf16, 2 * total),
        shape(cols),
        shape(cols),
        shape(cols),
        shape(cols),
        shape(rows),
        shape(rows),
    )
    *selectors, lower, upper, primal, cost, dual, rhs = pl.pallas_call(
        functools.partial(prep_kernel, chunks),
        out_shape=outs,
        in_specs=[
            pl.BlockSpec(memory_space=pltpu.SMEM if value is tile_count else pltpu.HBM)
            for value in inputs
        ],
        out_specs=tuple(vmem(len(outs))),
        scratch_shapes=[
            pltpu.VMEM((kept, size, size), f32),
            pltpu.VMEM((1, total), jnp.int32),
            pltpu.VMEM((1, total), jnp.int32),
            pltpu.VMEM(var_class.shape, jnp.int32),
            pltpu.VMEM((1, lower_table.shape[0]), f32),
            pltpu.VMEM((1, upper_table.shape[0]), f32),
            pltpu.SemaphoreType.DMA((chunks + 10,)),
        ],
        compiler_params=pltpu.CompilerParams(vmem_limit_bytes=16 << 20),
        cost_estimate=pl.CostEstimate(
            flops=4 * total * size * size,
            bytes_accessed=8 * total * size * size,
            transcendentals=0,
        ),
        name="prep",
    )(
        *(
            value if value is tile_count else pltpu.with_memory_space_constraint(value, pltpu.HBM)
            for value in inputs
        )
    )
    state = (*selectors, lower, upper, cost, tile_count)
    scratch = [pltpu.VMEM((extra, size), f32)]

    primal_1, window = kernel(
        first_kernel,
        (shape(cols), shape(3 * rows)),
        (*state, primal, dual, rhs, forth, reverse),
        limit=16 << 20,
        passes=2,
        scratch=scratch,
    )
    window, near, far = kernel(
        fold_kernel, (shape(3 * rows), shape(2 * rows), shape(rows)), group_sum(window)
    )
    near = lax.ppermute(near, AXES, ring(1))
    far = lax.ppermute(far, AXES, ring(2))
    (sent,) = kernel(side_kernel, (shape(2 * rows),), (window, near, far))
    got = swap(sent, 1)
    primal_2, window, dual_1 = kernel(
        later_kernel,
        (shape(cols), shape(3 * rows), shape(rows)),
        (*state, primal_1, rhs, window, sent, got),
        limit=16 << 20,
        passes=2,
        scratch=scratch,
    )
    own, forth, reverse = kernel(
        last_fold_kernel, (shape(rows),) * 3, group_sum(window)
    )
    forth, reverse = exchange(forth, reverse)
    primal_2, primal_mean = kernel(
        emit_kernel, (shape(cols), shape(cols)), (primal_1, primal_2)
    )
    even = lax.rem(tm, 2) == 0
    above = jnp.where(tm >= 1, jnp.where(even, forth, reverse), 0.0)
    below = jnp.where(tm + 1 < times, jnp.where(even, reverse, forth), 0.0)
    dual_2 = jnp.maximum(own + (above + below), 0.0)
    return primal_2, dual_2, primal_mean, (dual_1 + dual_2) / ITERS


def solution(mesh):
    groups, times = mesh.shape["grp"], mesh.shape["tm"]
    return jax.shard_map(
        functools.partial(body, groups, times),
        mesh=mesh,
        in_specs=(
            P(("grp", "tm"), None),
            P("tm", None),
            P(("grp", "tm"), None),
            P("tm", None),
            P(("grp", "tm"), None, None),
            P(("grp", "tm")),
            P(("grp", "tm")),
            P(("grp", "tm")),
            P(("grp", "tm"), None),
            P(),
            P(),
        ),
        out_specs=(P(("grp", "tm"), None), P("tm", None), P(("grp", "tm"), None), P("tm", None)),
        check_vma=False,
    )
```
